128 devices in a mesh: tmpl: 16 (over z, y_hi, core), chan: 8 (over y_lo, x).
Axes of the slice: x: 4, y: 4 (y_hi: 2, y_lo: 2; y = y_hi * 2 + y_lo), z: 4, core: 2. Of those that a mesh axis runs over, the one named last changes fastest.
Arguments:
- data: bfloat16 [16, 96, 2304], P('tmpl', 'chan')
- templates: bfloat16 [4096, 96, 200], P('tmpl', 'chan')
- counts: int32 [16], P('tmpl'), may hold values from 32 to 256, as said below
- owners: int32 [3], replicated, may hold values from 0 to 15
Outputs:
- traces: float32 [4096, 3, 2048], P('tmpl', None, 'chan')
The draws below stay inside these ranges and needn't reach their ends.
Inputs may be any that keep to these rules, and one draw needn't show every extreme that they name: `counts`: every count is a multiple of 32; some index of tmpl holds exactly 256 live slots.
All inputs are finite; a program needn't handle non-finite values.
Results may differ from the reference program's by a relative error of at most 0.0041.
Values may be sent and summed in bfloat16 or wider, within the bound.
A program may use at most 128 MiB of HBM per device.

```python
import math
import jax
import jax.numpy as jnp
from jax import lax

C = 96
W = 200
NB = 3
LO = 2048
K_CAP = 256
TB = 32
LB = 2304
KTOT = 4096
N_TMPL = 16


def draw_data(key, part):
    keys = jax.random.split(key, 3)
    shape = (N_TMPL, C, LB)
    base = jax.random.normal(keys[0], shape, jnp.float32)
    chan_scale = jnp.exp(jax.random.uniform(keys[1], (N_TMPL, C, 1), jnp.float32) * math.log(10.0))
    time_scale = jnp.exp(jax.random.uniform(keys[2], (N_TMPL, 1, LB), jnp.float32) * math.log(10.0))
    return (base * chan_scale * time_scale).astype(jnp.bfloat16)


def draw_templates(key, part):
    keys = jax.random.split(key, 3)
    shape = (KTOT, C, W)
    base = jax.random.normal(keys[0], shape, jnp.float32)
    row_scale = jnp.exp(jax.random.uniform(keys[1], (KTOT, C, 1), jnp.float32) * math.log(10.0))
    sample_scale = jnp.exp(jax.random.uniform(keys[2], (KTOT, 1, W), jnp.float32) * math.log(10.0))
    return (base * row_scale * sample_scale).astype(jnp.bfloat16)


def draw_counts(key, part):
    keys = jax.random.split(key, 2)
    shifts = jax.random.randint(keys[0], (N_TMPL,), 0, 4)
    units = jnp.right_shift(jnp.full((N_TMPL,), K_CAP // TB, jnp.int32), shifts.astype(jnp.int32))
    fullest = jax.random.randint(keys[1], (), 0, N_TMPL)
    units = jnp.where(jnp.arange(N_TMPL, dtype=jnp.int32) == fullest, K_CAP // TB, units)
    return (units * TB).astype(jnp.int32)


def setup_inputs(seed: int = 0) -> dict:
    key_list = jax.random.split(jax.random.key(seed), 5)
    data = draw_data(jax.random.fold_in(key_list[4], 71), 0)
    templates = draw_templates(jax.random.fold_in(key_list[4], 71), 0)
    counts = draw_counts(jax.random.fold_in(key_list[4], 71), 0)
    owners = jax.random.randint(key_list[3], (NB,), 0, N_TMPL).astype(jnp.int32)
    return {"data": data, "templates": templates, "counts": counts, "owners": owners}


eps_value = 1e-06

def normalize_templates(templates):
    values = templates.astype(jnp.float32)
    spread = jnp.sqrt(lax.optimization_barrier(jnp.mean(values * values, axis=-1, keepdims=True)) + eps_value)
    scaled = (values / (spread * math.sqrt(values.shape[-1]))).astype(jnp.bfloat16)
    return scaled.reshape(values.shape[0], -1)

def scaled_windows(segment, window_len, lag_count):
    rows = segment.shape[0]
    length = segment.shape[1]
    period = length - 1
    tiled = jnp.tile(segment[:, :period], (1, window_len + 1))
    windows = tiled[:, :window_len * length].reshape(rows, window_len, length)[:, :, :lag_count].astype(jnp.float32)
    spread = jnp.sqrt(lax.optimization_barrier(jnp.mean(windows * windows, axis=1, keepdims=True)) + eps_value)
    scaled = (windows / (spread * math.sqrt(window_len))).astype(jnp.bfloat16)
    return scaled.reshape(-1, lag_count)

def reference(data, templates, counts, owners):
    normed = normalize_templates(templates)
    slots = jnp.arange(KTOT, dtype=jnp.int32)
    holder = slots // K_CAP
    live = slots % K_CAP < counts[holder]
    results = []
    for number in range(NB):
        segment = lax.dynamic_index_in_dim(data, owners[number], 0, keepdims=False)
        scaled = scaled_windows(segment, W, LO)
        corr = jnp.dot(normed, scaled, preferred_element_type=jnp.float32)
        results.append(jnp.where(live[:, None], corr, jnp.float32(0.0)))
    return jnp.stack(results, axis=1)
```

```python
import math

import jax
import jax.numpy as jnp
from jax import lax
from jax.experimental import pallas as pl
from jax.experimental.pallas import tpu as pltpu
from jax.sharding import PartitionSpec as P

W = 200
WP = 208
NB = 3
LO = 2048
C = 12
LB = 2304
K = 256
KD = C * WP
NS = 256
NC = NB * NS
EPS = 1e-06
MESH = pl.DeviceIdType.MESH

A = (0, 112)
AH = ((0, 64), (64, 112))
B = (112, 256)
BH = ((192, 256), (112, 192))
F32 = jnp.float32
BF16 = jnp.bfloat16


def rows(span, base=0):
    return pl.ds(span[0] - base, span[1] - span[0])


def kernel(
    owners_ref, data_ref, tmpl_ref, out_ref,
    arch, shifts, base, inv, win, part, y_out, y_in, xo, xi, yb_out, yb_in,
    g_send, g_recv, y_send, y_recv, x_send, x_recv,
):
    tm = lax.axis_index("tmpl")
    ch = lax.axis_index("chan")
    z, yh, core = tm // 4, lax.rem(tm // 2, 2), lax.rem(tm, 2)
    yl, x = ch // 4, lax.rem(ch, 4)

    def tmpl_at(dz, dyh, dcore):
        return lax.rem(z + dz, 4) * 4 + lax.rem(yh + dyh, 2) * 2 + lax.rem(core + dcore, 2)

    def chan_at(dyl, dx):
        return lax.rem(yl + dyl, 2) * 4 + lax.rem(x + dx, 4)

    hops = [(dz, dyh) for dz in range(4) for dyh in range(2) if dz or dyh]
    x_dev = {-1: {"tmpl": tm, "chan": chan_at(0, 3)}, 1: {"tmpl": tm, "chan": chan_at(0, 1)}}
    y_dev = {"tmpl": tm, "chan": chan_at(1, 0)}
    mate = {"tmpl": tmpl_at(0, 0, 1), "chan": ch}

    barrier = pltpu.get_barrier_semaphore()
    peers = [mate, y_dev, x_dev[-1], x_dev[1]]
    peers += [{"tmpl": tmpl_at(dz, dyh, 0), "chan": ch} for dz, dyh in hops]
    for peer in peers:
        pl.semaphore_signal(barrier, inc=1, device_id=peer, device_id_type=MESH)
    pl.semaphore_wait(barrier, len(peers))

    sends = []
    for n, (dz, dyh) in enumerate(hops):
        copy = pltpu.make_async_remote_copy(
            data_ref, arch.at[tm], g_send.at[n], g_recv.at[n],
            device_id={"tmpl": tmpl_at(dz, dyh, 0), "chan": ch}, device_id_type=MESH)
        copy.start()
        sends.append(copy)
    copy = pltpu.make_async_remote_copy(
        data_ref, arch.at[tm], g_send.at[7], g_recv.at[7], device_id=mate, device_id_type=MESH)
    copy.start()
    sends.append(copy)
    arch[tm] = data_ref[...]
    forwards = []
    for n, (dz, dyh) in enumerate(hops):
        source = tmpl_at((4 - dz) % 4, dyh, 0)
        sends[n].wait_recv()
        copy = pltpu.make_async_remote_copy(
            arch.at[source], arch.at[source], g_send.at[8 + n], g_recv.at[8 + n],
            device_id=mate, device_id_type=MESH)
        copy.start()
        forwards.append(copy)
    for copy in sends[7:] + forwards:
        copy.wait_recv()

    for b in range(NB):
        seg = arch[owners_ref[b]].astype(F32)
        seg = jnp.concatenate([seg, jnp.zeros((4, LB), F32)], axis=0)
        for s in range(16):
            turned = pltpu.roll(seg, LB - s, 1) if s else seg
            for n in range(LB // 128):
                shifts[n, s * 48 + b * 16 : s * 48 + b * 16 + 16, :] = (
                    turned[:, n * 128 : n * 128 + 128])
        sums = {1: seg * seg}
        for n in (1, 2, 4, 8, 16, 32, 64):
            sums[2 * n] = sums[n] + pltpu.roll(sums[n], LB - n, 1)
        energy = (sums[128] + pltpu.roll(sums[64], LB - 128, 1)
                  + pltpu.roll(sums[8], LB - 192, 1))[:, :LO]
        inv[b] = 1.0 / (jnp.sqrt(energy * (1.0 / W) + EPS) * math.sqrt(W))
    for b in range(NB):
        for c in range(C):
            for n in range(LB // 128):
                base[b * C + c, :, n * 128 : n * 128 + 128] = (
                    shifts[n, pl.ds(b * 16 + c, 16, stride=48), :].astype(BF16))

    def remote(src, dst, send, recv, device):
        return pltpu.make_async_remote_copy(
            src, dst, send, recv, device_id=device, device_id_type=MESH)

    def y_copy(n):
        return remote(y_out.at[n], y_in.at[n], y_send.at[n], y_recv.at[n], y_dev)

    def yb_copy():
        return remote(yb_out, yb_in, y_send.at[4], y_recv.at[4], y_dev)

    def x_span(t, half):
        return AH[half] if t == 2 else BH[half]

    def x_copy(t, kind, half):
        span = rows(x_span(t, half))
        direction = -1 if half == 0 else 1
        if kind == 2:
            direction = -direction
        n = (t * 3 + kind) * 2 + half
        slot = min(t, 1) if t < 2 else 0
        return remote(
            xo.at[slot, kind, span], xi.at[slot, kind, span],
            x_send.at[n], x_recv.at[n], x_dev[direction])

    def x_slot(t):
        return min(t, 1) if t < 2 else 0

    def x_put(t, kind, half, value):
        xo[x_slot(t), kind, rows(x_span(t, half))] = value.astype(BF16)
        x_copy(t, kind, half).start()

    def x_got(t, kind, half):
        x_copy(t, kind, half).wait_recv()
        return xi[x_slot(t), kind, rows(x_span(t, half))].astype(F32)

    def own(n, span):
        return part[n, rows(span)]

    def local(t, n, half):
        span = x_span(t, half)
        if t == 2:
            return own(n, span) + y_in[n - 4, rows(span)].astype(F32)
        return own(n, span)

    def send_far(t, n):
        for half in (0, 1):
            x_put(t, 0, half, local(t, n, half))

    def send_direct(t, n, half):
        x_put(t, 2, half, local(t, n, half))

    def send_relay(t, n, half):
        x_put(t, 1, half, local(t, n, half) + x_got(t, 0, half))

    def total(t, n, half):
        return local(t, n, half) + x_got(t, 1, half) + x_got(t, 2, half)

    def y_first(n):
        y_out[n] = own(n, A).astype(BF16)
        y_copy(n).start()

    def after_0():
        y_first(0)
        send_far(0, 0)

    def after_1():
        y_first(1)
        send_direct(0, 1, 0)

    def after_2():
        y_first(2)
        send_direct(0, 2, 1)
        send_relay(0, 1, 1)
        send_relay(0, 2, 0)

    def after_3():
        y_first(3)

    def after_4():
        send_far(1, 4)
        y_copy(0).wait_recv()
        send_far(2, 4)

    def after_5():
        send_direct(1, 5, 0)
        y_copy(1).wait_recv()
        send_direct(2, 5, 0)
        for half in (0, 1):
            yb_out[rows(x_span(0, half), B[0])] = total(0, 3, half).astype(BF16)
        yb_copy().start()

    def after_6():
        send_direct(1, 6, 1)
        y_copy(2).wait_recv()
        send_direct(2, 6, 1)
        send_relay(1, 5, 1)
        send_relay(1, 6, 0)
        send_relay(2, 5, 1)
        send_relay(2, 6, 0)

    actions = [after_0, after_1, after_2, after_3, after_4, after_5, after_6]

    def chunk(n, carry):
        step = lax.rem(n, 4)
        dx = jnp.where(step == 0, 2, jnp.where(step == 1, 1, jnp.where(step == 2, 3, 0)))
        dest = lax.rem(yl + 1 + n // 4, 2) * 4 + lax.rem(x + dx, 4)
        lag = pl.multiple_of(dest * NS, NS)

        def channel(c, carry):
            row = pl.multiple_of(c * WP, 16)
            for b in range(NB):
                cols = slice(b * NS, (b + 1) * NS)
                wide = base[b * C + c, :, pl.ds(lag, 512)]
                scale = inv[b, pl.ds(c, 1), pl.ds(lag, NS)]
                for r in range(8):
                    turned = pltpu.roll(wide, 512 - 16 * r, 1) if r else wide
                    turned = turned.astype(F32)
                    win[pl.ds(row + 16 * r, 16), cols] = (turned[:, :NS] * scale).astype(BF16)
                    if r < 5:
                        win[pl.ds(row + 16 * r + 128, 16), cols] = (
                            turned[:, 128 : 128 + NS] * scale).astype(BF16)
            return carry

        lax.fori_loop(0, C, channel, 0)
        part[n] = jnp.dot(tmpl_ref[...], win[...], preferred_element_type=F32)
        for m, action in enumerate(actions):
            pl.when(n == m)(action)
        return carry

    lax.fori_loop(0, 8, chunk, 0)

    y_copy(3).wait_recv()
    for half in (0, 1):
        out_ref[rows(AH[half])] = total(2, 7, half)
    yb_copy().wait_recv()
    for half in (0, 1):
        span = x_span(1, half)
        out_ref[rows(span)] = total(1, 7, half) + yb_in[rows(span, B[0])].astype(F32)

    for copy in sends + forwards:
        copy.wait_send()
    for n in range(4):
        y_copy(n).wait_send()
    yb_copy().wait_send()
    for t in range(3):
        for kind in range(3):
            for half in (0, 1):
                x_copy(t, kind, half).wait_send()


def normalize_templates(templates):
    values = templates.astype(F32)
    spread = jnp.sqrt(jnp.mean(values * values, axis=-1, keepdims=True) + EPS)
    scaled = (values / (spread * math.sqrt(W))).astype(BF16)
    return jnp.pad(scaled, ((0, 0), (0, 0), (0, WP - W))).reshape(K, KD)


def body(data, templates, counts, owners):
    normed = normalize_templates(templates)
    vmem = pl.BlockSpec(memory_space=pltpu.VMEM)
    dma = pltpu.SemaphoreType.DMA
    traces = pl.pallas_call(
        kernel,
        out_shape=jax.ShapeDtypeStruct((K, NC), F32),
        in_specs=[pl.BlockSpec(memory_space=pltpu.SMEM), vmem, vmem],
        out_specs=vmem,
        scratch_shapes=[
            pltpu.VMEM((16, C, LB), BF16),
            pltpu.VMEM((LB // 128, 16 * 48, 128), F32),
            pltpu.VMEM((NB * C, 16, LB), BF16),
            pltpu.VMEM((NB, 16, LO), F32),
            pltpu.VMEM((KD, NC), BF16),
            pltpu.VMEM((8, K, NC), F32),
            pltpu.VMEM((4, A[1], NC), BF16),
            pltpu.VMEM((4, A[1], NC), BF16),
            pltpu.VMEM((2, 3, K, NC), BF16),
            pltpu.VMEM((2, 3, K, NC), BF16),
            pltpu.VMEM((B[1] - B[0], NC), BF16),
            pltpu.VMEM((B[1] - B[0], NC), BF16),
            dma((15,)), dma((15,)), dma((5,)), dma((5,)), dma((18,)), dma((18,)),
        ],
        compiler_params=pltpu.CompilerParams(
            collective_id=0, has_side_effects=True, vmem_limit_bytes=60 << 20),
    )(owners, data[0], normed)
    live = jnp.arange(K, dtype=jnp.int32) < counts[0]
    return jnp.where(live[:, None, None], traces.reshape(K, NB, NS), 0.0)


def solution(mesh):
    placed = (P("tmpl", "chan", None), P("tmpl", "chan", None), P("tmpl"), P())
    return jax.shard_map(
        body, mesh=mesh, in_specs=placed, out_specs=P("tmpl", None, "chan"), check_vma=False
    )
```

```python
import math

import jax
import jax.numpy as jnp
from jax import lax
from jax.experimental import pallas as pl
from jax.experimental.pallas import tpu as pltpu
from jax.sharding import PartitionSpec as P

W = 200
WP = 208
NB = 3
LO = 2048
C = 12
CH = C // 2
LB = 2304
K = 256
KH = CH * WP
NS = 256
NC = NB * NS
EPS = 1e-06
MESH = pl.DeviceIdType.MESH
GROUPS = (512, 1280, 1280)

A = (0, 112)
AH = ((0, 64), (64, 112))
B = (112, 256)
BH = ((192, 256), (112, 192))
F32 = jnp.float32
BF16 = jnp.bfloat16


def rows(span, base=0):
    return pl.ds(span[0] - base, span[1] - span[0])


def kernel(
    owners_ref, data_ref, tmpl_ref, out_ref,
    arch0, arch1, arch2, columns, lhs0, lhs1, shifts, base, inv, win0, win1, part,
    y_out, y_in, xo, xi, yb_out, yb_in,
    g_send, g_recv, y_send, y_recv, x_send, x_recv,
):
    tm = lax.axis_index("tmpl")
    ch = lax.axis_index("chan")
    z, yh, core = tm // 4, lax.rem(tm // 2, 2), lax.rem(tm, 2)
    yl, x = ch // 4, lax.rem(ch, 4)
    e = 1 - 2 * core

    def block(dz, dyh):
        return lax.rem(z + 4 + dz * e, 4) * 4 + lax.rem(yh + dyh, 2) * 2 + core

    def chan_at(dyl, dx):
        return lax.rem(yl + dyl, 2) * 4 + lax.rem(x + dx, 4)

    ahead = {"tmpl": block(1, 0), "chan": ch}
    behind = {"tmpl": block(-1, 0), "chan": ch}
    across = {"tmpl": block(0, 1), "chan": ch}
    mate = {"tmpl": z * 4 + yh * 2 + (1 - core), "chan": ch}
    x_dev = {-1: {"tmpl": tm, "chan": chan_at(0, 3)}, 1: {"tmpl": tm, "chan": chan_at(0, 1)}}
    y_dev = {"tmpl": tm, "chan": chan_at(1, 0)}

    barrier = pltpu.get_barrier_semaphore()
    peers = [mate, ahead, behind, across, y_dev, x_dev[-1], x_dev[1]]
    for peer in peers:
        pl.semaphore_signal(barrier, inc=1, device_id=peer, device_id_type=MESH)
    pl.semaphore_wait(barrier, len(peers))

    def remote(src, dst, send, recv, device):
        return pltpu.make_async_remote_copy(
            src, dst, send, recv, device_id=device, device_id_type=MESH)

    archs = (arch0, arch1, arch2)
    first = (1 - yl) * 4 + lax.rem(x + 2, 4)
    starts = [
        pl.multiple_of(first * NS, NS),
        pl.multiple_of((1 - yl) * 1024, 1024),
        pl.multiple_of(yl * 1024, 1024),
    ]
    targets = (ahead, behind, across, ahead, ahead, behind, ahead, mate) + (mate,) * 7
    carried = (None, None, None, (-1, 0), (0, 1), (0, 1), (-1, 1), None)
    carried += ((-1, 0), (1, 0), (0, 1), (-2, 0), (-1, 1), (1, 1), (-2, 1))

    def g_copy(g, m):
        if carried[m] is None:
            src = data_ref.at[:, pl.ds(starts[g], GROUPS[g])]
            dst = archs[g].at[tm]
        else:
            src = dst = archs[g].at[block(*carried[m])]
        return remote(src, dst, g_send.at[g, m], g_recv.at[g, m], targets[m])

    def g_start(g):
        for m in (2, 0, 1, 7):
            g_copy(g, m).start()
        archs[g][tm] = data_ref[:, pl.ds(starts[g], GROUPS[g])]

    def g_pass(g, m, on):
        g_copy(g, m).wait_recv()
        for k in on:
            g_copy(g, k).start()

    def g_stage1(g):
        g_pass(g, 0, (3, 8))
        g_pass(g, 1, (9,))
        g_pass(g, 2, (4, 5, 10))

    def g_stage2(g):
        g_pass(g, 3, (11,))
        g_pass(g, 4, (6, 12))
        g_pass(g, 5, (13,))

    def g_stage3(g):
        g_pass(g, 6, (14,))

    def g_finish(g):
        for m in range(7, 15):
            g_copy(g, m).wait_recv()
        width = GROUPS[g]
        for b in range(NB):
            seg = archs[g][owners_ref[b]].astype(F32)
            seg = jnp.concatenate([seg, jnp.zeros((4, width), F32)], axis=0)
            for s in range(16):
                turned = pltpu.roll(seg, width - s, 1) if s else seg
                for n in range(width // 128):
                    shifts[n, s * 48 + b * 16 : s * 48 + b * 16 + 16, :] = (
                        turned[:, n * 128 : n * 128 + 128])
            sums = {1: seg * seg}
            for n in (1, 2, 4, 8, 16, 32, 64):
                sums[2 * n] = sums[n] + pltpu.roll(sums[n], width - n, 1)
            energy = (sums[128] + pltpu.roll(sums[64], width - 128, 1)
                      + pltpu.roll(sums[8], width - 192, 1))[:, : width - 256]
            inv[b, :, pl.ds(starts[g], width - 256)] = (
                1.0 / (jnp.sqrt(energy * (1.0 / W) + EPS) * math.sqrt(W)))
        for b in range(NB):
            for c in range(C):
                for n in range(width // 128):
                    base[b * C + c, :, pl.ds(starts[g] + n * 128, 128)] = (
                        shifts[n, pl.ds(b * 16 + c, 16, stride=48), :])

    g_start(0)
    g_start(1)

    for half, lhs in ((0, lhs0), (1, lhs1)):
        for c in range(CH):
            values = tmpl_ref[half * CH + c].astype(F32)
            power = jnp.sum(values * values, axis=0, keepdims=True) * (1.0 / W)
            scaled = values * (1.0 / (jnp.sqrt(power + EPS) * math.sqrt(W)))
            columns[c * WP : c * WP + W, :] = scaled
            columns[c * WP + W : (c + 1) * WP, :] = jnp.zeros((WP - W, K), F32)
        lhs[...] = columns[...].T.astype(BF16)

    g_stage1(0)
    g_stage2(0)
    g_stage1(1)
    g_stage3(0)
    g_stage2(1)
    g_start(2)
    g_finish(0)

    def y_copy(n):
        return remote(y_out.at[n], y_in.at[n], y_send.at[n], y_recv.at[n], y_dev)

    def yb_copy():
        return remote(yb_out, yb_in, y_send.at[4], y_recv.at[4], y_dev)

    def x_span(t, half):
        return AH[half] if t == 2 else BH[half]

    def x_slot(t):
        return t % 2

    def x_copy(t, kind, half):
        span = rows(x_span(t, half))
        direction = -1 if half == 0 else 1
        if kind == 2:
            direction = -direction
        n = (t * 3 + kind) * 2 + half
        return remote(
            xo.at[x_slot(t), kind, span], xi.at[x_slot(t), kind, span],
            x_send.at[n], x_recv.at[n], x_dev[direction])

    def x_put(t, kind, half, value):
        xo[x_slot(t), kind, rows(x_span(t, half))] = value.astype(BF16)
        x_copy(t, kind, half).start()

    def x_got(t, kind, half):
        x_copy(t, kind, half).wait_recv()
        return xi[x_slot(t), kind, rows(x_span(t, half))].astype(F32)

    def own(n, span):
        return part[n, rows(span)]

    def local(t, n, half):
        span = x_span(t, half)
        if t == 2:
            return own(n, span) + y_in[n - 4, rows(span)].astype(F32)
        return own(n, span)

    def send_far(t, n):
        for half in (0, 1):
            x_put(t, 0, half, local(t, n, half))

    def send_direct(t, n, half):
        x_put(t, 2, half, local(t, n, half))

    def send_relay(t, n, half):
        x_put(t, 1, half, local(t, n, half) + x_got(t, 0, half))

    def total(t, n, half):
        return local(t, n, half) + x_got(t, 1, half) + x_got(t, 2, half)

    def y_first(n):
        y_out[n] = own(n, A).astype(BF16)
        y_copy(n).start()

    def between_0():
        g_stage3(1)
        g_finish(1)

    def between_1():
        g_stage1(2)

    def between_2():
        g_stage2(2)

    def between_3():
        g_stage3(2)
        g_finish(2)

    def after_0():
        y_first(0)
        send_far(0, 0)

    def after_1():
        y_first(1)
        send_direct(0, 1, 0)

    def after_2():
        y_first(2)
        send_direct(0, 2, 1)

    def after_3():
        y_first(3)

    def after_4():
        send_far(1, 4)
        send_relay(0, 1, 1)
        send_relay(0, 2, 0)

    def after_5():
        send_direct(1, 5, 0)
        y_copy(0).wait_recv()
        send_far(2, 4)

    def after_6():
        send_direct(1, 6, 1)

    betweens = [between_0, between_1, between_2, between_3]
    actions = [after_0, after_1, after_2, after_3, after_4, after_5, after_6]

    def dest(n):
        step = lax.rem(n, 4)
        dx = jnp.where(step == 0, 2, jnp.where(step == 1, 1, jnp.where(step == 2, 3, 0)))
        return lax.rem(yl + 1 + n // 4, 2) * 4 + lax.rem(x + dx, 4)

    def build(win, half, n):
        lag = pl.multiple_of(dest(n) * NS, NS)
        for c in range(CH):
            for b in range(NB):
                cols = slice(b * NS, (b + 1) * NS)
                wide = base[b * C + half * CH + c, :, pl.ds(lag, 512)]
                scale = inv[b, half * CH + c : half * CH + c + 1, pl.ds(lag, NS)]
                for r in range(8):
                    turned = pltpu.roll(wide, 512 - 16 * r, 1) if r else wide
                    row = c * WP + 16 * r
                    win[row : row + 16, cols] = (turned[:, :NS] * scale).astype(BF16)
                    if r < 5:
                        win[row + 128 : row + 144, cols] = (
                            turned[:, 128 : 128 + NS] * scale).astype(BF16)

    build(win0, 0, 0)

    def chunk(n, carry):
        build(win1, 1, n)
        part[n] = jnp.dot(lhs0[...], win0[...], preferred_element_type=F32)
        for m, action in enumerate(betweens):
            pl.when(n == m)(action)
        build(win0, 0, jnp.minimum(n + 1, 7))
        part[n] += jnp.dot(lhs1[...], win1[...], preferred_element_type=F32)
        for m, action in enumerate(actions):
            pl.when(n == m)(action)
        return carry

    lax.fori_loop(0, 8, chunk, 0)

    send_relay(1, 5, 1)
    send_relay(1, 6, 0)
    y_copy(1).wait_recv()
    send_direct(2, 5, 0)
    send_relay(2, 5, 1)
    for half in (0, 1):
        yb_out[rows(x_span(0, half), B[0])] = total(0, 3, half).astype(BF16)
    yb_copy().start()
    y_copy(2).wait_recv()
    send_direct(2, 6, 1)
    send_relay(2, 6, 0)

    def finish(span, value):
        for b in range(NB):
            out_ref[b, rows(span)] = value[:, b * NS : (b + 1) * NS]

    y_copy(3).wait_recv()
    for half in (0, 1):
        finish(AH[half], total(2, 7, half))
    yb_copy().wait_recv()
    for half in (0, 1):
        span = x_span(1, half)
        finish(span, total(1, 7, half) + yb_in[rows(span, B[0])].astype(F32))

    for g in range(3):
        for m in range(15):
            g_copy(g, m).wait_send()
    for n in range(4):
        y_copy(n).wait_send()
    yb_copy().wait_send()
    for t in range(3):
        for kind in range(3):
            for half in (0, 1):
                x_copy(t, kind, half).wait_send()


def body(data, templates, counts, owners):
    vmem = pl.BlockSpec(memory_space=pltpu.VMEM)
    dma = pltpu.SemaphoreType.DMA
    traces = pl.pallas_call(
        kernel,
        out_shape=jax.ShapeDtypeStruct((NB, K, NS), F32),
        in_specs=[pl.BlockSpec(memory_space=pltpu.SMEM), vmem, vmem],
        out_specs=vmem,
        scratch_shapes=[
            pltpu.VMEM((16, C, GROUPS[0]), BF16),
            pltpu.VMEM((16, C, GROUPS[1]), BF16),
            pltpu.VMEM((16, C, GROUPS[2]), BF16),
            pltpu.VMEM((KH, K), F32),
            pltpu.VMEM((K, KH), BF16),
            pltpu.VMEM((K, KH), BF16),
            pltpu.VMEM((GROUPS[1] // 128, 16 * 48, 128), F32),
            pltpu.VMEM((NB * C, 16, LB), F32),
            pltpu.VMEM((NB, 16, LO), F32),
            pltpu.VMEM((KH, NC), BF16),
            pltpu.VMEM((KH, NC), BF16),
            pltpu.VMEM((8, K, NC), F32),
            pltpu.VMEM((4, A[1], NC), BF16),
            pltpu.VMEM((4, A[1], NC), BF16),
            pltpu.VMEM((2, 3, K, NC), BF16),
            pltpu.VMEM((2, 3, K, NC), BF16),
            pltpu.VMEM((B[1] - B[0], NC), BF16),
            pltpu.VMEM((B[1] - B[0], NC), BF16),
            dma((3, 15)), dma((3, 15)), dma((5,)), dma((5,)), dma((18,)), dma((18,)),
        ],
        compiler_params=pltpu.CompilerParams(
            collective_id=0, has_side_effects=True, vmem_limit_bytes=60 << 20),
    )(owners, data[0], jnp.transpose(templates, (1, 2, 0)))
    live = jnp.arange(K, dtype=jnp.int32) < counts[0]
    return jnp.transpose(jnp.where(live[None, :, None], traces, 0.0), (1, 0, 2))


def solution(mesh):
    placed = (P("tmpl", "chan", None), P("tmpl", "chan", None), P("tmpl"), P())
    return jax.shard_map(
        body, mesh=mesh, in_specs=placed, out_specs=P("tmpl", None, "chan"), check_vma=False
    )
```

```python
import math

import jax
import jax.numpy as jnp
from jax import lax
from jax.experimental import pallas as pl
from jax.experimental.pallas import tpu as pltpu
from jax.sharding import PartitionSpec as P

W = 200
NB = 3
LO = 2048
C = 12
CG = C // 4
LB = 2304
K = 256
KR = 16 * CG
PHASES = ((0, 16), (16, 32))
TAPS = tuple(tuple(g for lo in (a, a + 32) for g in range(lo, lo + 16) if 4 * g < W) for a, _ in PHASES)
KH = tuple(len(taps) * KR for taps in TAPS)
NS = 256
NC = NB * NS
EPS = 1e-06
MESH = pl.DeviceIdType.MESH
GROUPS = (512, 1280, 1280)

A = (0, 112)
AH = ((0, 64), (64, 112))
B = (112, 256)
BH = ((192, 256), (112, 192))
F32 = jnp.float32
BF16 = jnp.bfloat16


def rows(span, base=0):
    return pl.ds(span[0] - base, span[1] - span[0])


def kernel(
    owners_ref, data_ref, tmpl_ref, out_ref,
    arch0, arch1, arch2, normed, columns, lhs0, lhs1, base, inv, band, win0, win1, part,
    y_out, y_in, xo, xi, yb_out, yb_in,
    g_send, g_recv, y_send, y_recv, x_send, x_recv,
):
    tm = lax.axis_index("tmpl")
    ch = lax.axis_index("chan")
    z, yh, core = tm // 4, lax.rem(tm // 2, 2), lax.rem(tm, 2)
    yl, x = ch // 4, lax.rem(ch, 4)
    e = 1 - 2 * core

    def block(dz, dyh):
        return lax.rem(z + 4 + dz * e, 4) * 4 + lax.rem(yh + dyh, 2) * 2 + core

    def chan_at(dyl, dx):
        return lax.rem(yl + dyl, 2) * 4 + lax.rem(x + dx, 4)

    ahead = {"tmpl": block(1, 0), "chan": ch}
    behind = {"tmpl": block(-1, 0), "chan": ch}
    across = {"tmpl": block(0, 1), "chan": ch}
    mate = {"tmpl": z * 4 + yh * 2 + (1 - core), "chan": ch}
    x_dev = {-1: {"tmpl": tm, "chan": chan_at(0, 3)}, 1: {"tmpl": tm, "chan": chan_at(0, 1)}}
    y_dev = {"tmpl": tm, "chan": chan_at(1, 0)}

    barrier = pltpu.get_barrier_semaphore()
    peers = [mate, ahead, behind, across, y_dev, x_dev[-1], x_dev[1]]
    for peer in peers:
        pl.semaphore_signal(barrier, inc=1, device_id=peer, device_id_type=MESH)
    pl.semaphore_wait(barrier, len(peers))

    def remote(src, dst, send, recv, device):
        return pltpu.make_async_remote_copy(
            src, dst, send, recv, device_id=device, device_id_type=MESH)

    archs = (arch0, arch1, arch2)
    first = (1 - yl) * 4 + lax.rem(x + 2, 4)
    starts = [
        pl.multiple_of(first * NS, NS),
        pl.multiple_of((1 - yl) * 1024, 1024),
        pl.multiple_of(yl * 1024, 1024),
    ]
    targets = (ahead, behind, across, ahead, ahead, behind, ahead, mate) + (mate,) * 7
    carried = (None, None, None, (-1, 0), (0, 1), (0, 1), (-1, 1), None)
    carried += ((-1, 0), (1, 0), (0, 1), (-2, 0), (-1, 1), (1, 1), (-2, 1))

    def g_copy(g, m):
        if carried[m] is None:
            src = data_ref.at[:, pl.ds(starts[g], GROUPS[g])]
            dst = archs[g].at[tm]
        else:
            src = dst = archs[g].at[block(*carried[m])]
        return remote(src, dst, g_send.at[g, m], g_recv.at[g, m], targets[m])

    def g_start(g):
        for m in (2, 0, 1, 7):
            g_copy(g, m).start()
        archs[g][tm] = data_ref[:, pl.ds(starts[g], GROUPS[g])]

    def g_pass(g, m, on):
        g_copy(g, m).wait_recv()
        for k in on:
            g_copy(g, k).start()

    def g_stage1(g):
        g_pass(g, 0, (3, 8))
        g_pass(g, 1, (9,))
        g_pass(g, 2, (4, 5, 10))

    def g_stage2(g):
        g_pass(g, 3, (11,))
        g_pass(g, 4, (6, 12))
        g_pass(g, 5, (13,))

    def g_stage3(g):
        g_pass(g, 6, (14,))

    def g_finish(g):
        for m in range(7, 15):
            g_copy(g, m).wait_recv()
        width = GROUPS[g]
        for b in range(NB):
            seg = archs[g][owners_ref[b]].astype(F32)
            seg = jnp.concatenate([seg, jnp.zeros((4, width), F32)], axis=0)
            small = seg * (1.0 / 256)
            power = jnp.minimum(small * small, 2.0**120)
            high = power.astype(BF16)
            low = (power - high.astype(F32)).astype(BF16)
            squares = jnp.concatenate([high, low], axis=0)
            for n in range(width // NS - 1):
                energy = jnp.dot(squares[:, n * NS : n * NS + 512], band[...],
                                 preferred_element_type=F32)
                mean = (energy[:16] + energy[16:]) * (65536.0 / W)
                scale = 1.0 / (jnp.sqrt(mean + EPS) * math.sqrt(W))
                for q in range(CG):
                    for s in range(4):
                        inv[b * CG + q, 4 * s : 4 * s + 4, pl.ds(starts[g] + n * NS, NS)] = (
                            scale[4 * q : 4 * q + 4])
            seg = seg.astype(BF16)
            for s in range(4):
                turned = pltpu.roll(seg, width - s, 1) if s else seg
                turned = turned.astype(F32)
                for q in range(CG):
                    base[b * CG + q, 4 * s : 4 * s + 4, pl.ds(starts[g], width)] = (
                        turned[4 * q : 4 * q + 4])

    g_start(0)
    g_start(1)

    sample = lax.broadcasted_iota(jnp.int32, (512, NS), 0)
    lag_of = lax.broadcasted_iota(jnp.int32, (512, NS), 1)
    inside = jnp.logical_and(sample >= lag_of, sample < lag_of + W)
    band[...] = jnp.where(inside, 1.0, 0.0).astype(BF16)

    for c in range(C):
        values = tmpl_ref[c].astype(F32)
        power = jnp.sum(values * values, axis=0, keepdims=True) * (1.0 / W)
        scaled = values * (1.0 / (jnp.sqrt(power + EPS) * math.sqrt(W)))
        for j in range(2):
            normed[j] = scaled[:, j * 128 : j * 128 + 128]
            for s in range(4):
                row = c // 4 * 16 + 4 * s + c % 4
                columns[j, pl.ds(row, W // 4, stride=KR), :] = (
                    normed[j, pl.ds(s, W // 4, stride=4), :])
    for lhs, (lo, hi) in ((lhs0, PHASES[0]), (lhs1, PHASES[1])):
        tail = min(hi + 32, W // 4)
        for j in range(2):
            band_rows = slice(j * 128, j * 128 + 128)
            cut = (hi - lo) * KR
            lhs[band_rows, :cut] = columns[j, lo * KR : hi * KR, :].T.astype(BF16)
            lhs[band_rows, cut:] = columns[j, (lo + 32) * KR : tail * KR, :].T.astype(BF16)

    g_stage1(0)
    g_stage2(0)
    g_stage1(1)
    g_stage3(0)
    g_stage2(1)
    g_start(2)
    g_finish(0)

    def y_copy(n):
        return remote(y_out.at[n], y_in.at[n], y_send.at[n], y_recv.at[n], y_dev)

    def yb_copy():
        return remote(yb_out, yb_in, y_send.at[4], y_recv.at[4], y_dev)

    def x_span(t, half):
        return AH[half] if t == 2 else BH[half]

    def x_slot(t):
        return t % 2

    def x_copy(t, kind, half):
        span = rows(x_span(t, half))
        direction = -1 if half == 0 else 1
        if kind == 2:
            direction = -direction
        n = (t * 3 + kind) * 2 + half
        return remote(
            xo.at[x_slot(t), kind, span], xi.at[x_slot(t), kind, span],
            x_send.at[n], x_recv.at[n], x_dev[direction])

    def x_put(t, kind, half, value):
        xo[x_slot(t), kind, rows(x_span(t, half))] = value.astype(BF16)
        x_copy(t, kind, half).start()

    def x_got(t, kind, half):
        x_copy(t, kind, half).wait_recv()
        return xi[x_slot(t), kind, rows(x_span(t, half))].astype(F32)

    def own(n, span):
        return part[n, rows(span)]

    def local(t, n, half):
        span = x_span(t, half)
        if t == 2:
            return own(n, span) + y_in[n - 4, rows(span)].astype(F32)
        return own(n, span)

    def send_far(t, n):
        for half in (0, 1):
            x_put(t, 0, half, local(t, n, half))

    def send_direct(t, n, half):
        x_put(t, 2, half, local(t, n, half))

    def send_relay(t, n, half):
        x_put(t, 1, half, local(t, n, half) + x_got(t, 0, half))

    def total(t, n, half):
        return local(t, n, half) + x_got(t, 1, half) + x_got(t, 2, half)

    def y_first(n):
        y_out[n] = own(n, A).astype(BF16)
        y_copy(n).start()

    def between_0():
        g_stage3(1)
        g_finish(1)

    def between_1():
        g_stage1(2)

    def between_2():
        g_stage2(2)

    def between_3():
        g_stage3(2)
        g_finish(2)

    def after_0():
        y_first(0)
        send_far(0, 0)

    def after_1():
        y_first(1)
        send_direct(0, 1, 0)

    def after_2():
        y_first(2)
        send_direct(0, 2, 1)

    def after_3():
        y_first(3)

    def after_4():
        send_far(1, 4)
        send_relay(0, 1, 1)
        send_relay(0, 2, 0)

    def after_5():
        send_direct(1, 5, 0)
        y_copy(0).wait_recv()
        send_far(2, 4)

    def after_6():
        send_direct(1, 6, 1)

    betweens = [between_0, between_1, between_2, between_3]
    actions = [after_0, after_1, after_2, after_3, after_4, after_5, after_6]

    def dest(n):
        step = lax.rem(n, 4)
        dx = jnp.where(step == 0, 2, jnp.where(step == 1, 1, jnp.where(step == 2, 3, 0)))
        return lax.rem(yl + 1 + n // 4, 2) * 4 + lax.rem(x + dx, 4)

    def build(win, half, n):
        lag = pl.multiple_of(dest(n) * NS, NS)
        taps = TAPS[half]
        for b in range(NB):
            cols = slice(b * NS, (b + 1) * NS)
            for q in range(CG):
                wide = base[b * CG + q, :, pl.ds(lag, 512)].astype(BF16)
                scale = inv[b * CG + q, :, pl.ds(lag, NS)]
                for p in range(*PHASES[half]):
                    turned = pltpu.roll(wide, 512 - 4 * p, 1) if p else wide
                    turned = turned.astype(F32)
                    row = taps.index(p) * KR + q * 16
                    win[row : row + 16, cols] = (turned[:, :NS] * scale).astype(BF16)
                    if p + 32 in taps:
                        row = taps.index(p + 32) * KR + q * 16
                        win[row : row + 16, cols] = (
                            turned[:, 128 : 128 + NS] * scale).astype(BF16)

    build(win0, 0, 0)

    def chunk(n, carry):
        build(win1, 1, n)
        part[n] = jnp.dot(lhs0[...], win0[...], preferred_element_type=F32)
        for m, action in enumerate(betweens):
            pl.when(n == m)(action)
        build(win0, 0, jnp.minimum(n + 1, 7))
        part[n] += jnp.dot(lhs1[...], win1[...], preferred_element_type=F32)
        for m, action in enumerate(actions):
            pl.when(n == m)(action)
        return carry

    lax.fori_loop(0, 8, chunk, 0)

    send_relay(1, 5, 1)
    send_relay(1, 6, 0)
    y_copy(1).wait_recv()
    send_direct(2, 5, 0)
    send_relay(2, 5, 1)
    for half in (0, 1):
        yb_out[rows(x_span(0, half), B[0])] = total(0, 3, half).astype(BF16)
    yb_copy().start()
    y_copy(2).wait_recv()
    send_direct(2, 6, 1)
    send_relay(2, 6, 0)

    def finish(span, value):
        for b in range(NB):
            out_ref[b, rows(span)] = value[:, b * NS : (b + 1) * NS]

    y_copy(3).wait_recv()
    for half in (0, 1):
        finish(AH[half], total(2, 7, half))
    yb_copy().wait_recv()
    for half in (0, 1):
        span = x_span(1, half)
        finish(span, total(1, 7, half) + yb_in[rows(span, B[0])].astype(F32))

    for g in range(3):
        for m in range(15):
            g_copy(g, m).wait_send()
    for n in range(4):
        y_copy(n).wait_send()
    yb_copy().wait_send()
    for t in range(3):
        for kind in range(3):
            for half in (0, 1):
                x_copy(t, kind, half).wait_send()


def body(data, templates, counts, owners):
    vmem = pl.BlockSpec(memory_space=pltpu.VMEM)
    dma = pltpu.SemaphoreType.DMA
    traces = pl.pallas_call(
        kernel,
        out_shape=jax.ShapeDtypeStruct((NB, K, NS), F32),
        in_specs=[pl.BlockSpec(memory_space=pltpu.SMEM), vmem, vmem],
        out_specs=vmem,
        scratch_shapes=[
            pltpu.VMEM((16, C, GROUPS[0]), BF16),
            pltpu.VMEM((16, C, GROUPS[1]), BF16),
            pltpu.VMEM((16, C, GROUPS[2]), BF16),
            pltpu.VMEM((2, W, 128), F32),
            pltpu.VMEM((2, W * C, 128), F32),
            pltpu.VMEM((K, KH[0]), BF16),
            pltpu.VMEM((K, KH[1]), BF16),
            pltpu.VMEM((NB * CG, 16, LB), F32),
            pltpu.VMEM((NB * CG, 16, LO), F32),
            pltpu.VMEM((512, NS), BF16),
            pltpu.VMEM((KH[0], NC), BF16),
            pltpu.VMEM((KH[1], NC), BF16),
            pltpu.VMEM((8, K, NC), F32),
            pltpu.VMEM((4, A[1], NC), BF16),
            pltpu.VMEM((4, A[1], NC), BF16),
            pltpu.VMEM((2, 3, K, NC), BF16),
            pltpu.VMEM((2, 3, K, NC), BF16),
            pltpu.VMEM((B[1] - B[0], NC), BF16),
            pltpu.VMEM((B[1] - B[0], NC), BF16),
            dma((3, 15)), dma((3, 15)), dma((5,)), dma((5,)), dma((18,)), dma((18,)),
        ],
        compiler_params=pltpu.CompilerParams(
            collective_id=0, has_side_effects=True, vmem_limit_bytes=60 << 20),
    )(owners, data[0], jnp.transpose(templates, (1, 2, 0)))
    live = jnp.arange(K, dtype=jnp.int32) < counts[0]
    return jnp.transpose(jnp.where(live[None, :, None], traces, 0.0), (1, 0, 2))


def solution(mesh):
    placed = (P("tmpl", "chan", None), P("tmpl", "chan", None), P("tmpl"), P())
    return jax.shard_map(
        body, mesh=mesh, in_specs=placed, out_specs=P("tmpl", None, "chan"), check_vma=False
    )
```

```python
import math

import jax
import jax.numpy as jnp
from jax import lax
from jax.experimental import pallas as pl
from jax.experimental.pallas import tpu as pltpu
from jax.sharding import PartitionSpec as P

W = 200
NB = 3
LO = 2048
C = 12
CG = C // 4
LB = 2304
K = 256
KR = 16 * CG
PHASES = ((0, 16), (16, 32))
TAPS = tuple(tuple(g for lo in (a, a + 32) for g in range(lo, lo + 16) if 4 * g < W) for a, _ in PHASES)
KH = tuple(len(taps) * KR for taps in TAPS)
NS = 256
NC = NB * NS
EPS = 1e-06
MESH = pl.DeviceIdType.MESH
GROUPS = (512, 1280, 1280)
MODES = ("chip", "chip", "tree")

A = (0, 112)
AH = ((0, 64), (64, 112))
B = (112, 256)
BH = ((192, 256), (112, 192))
F32 = jnp.float32
BF16 = jnp.bfloat16


def rows(span, base=0):
    return pl.ds(span[0] - base, span[1] - span[0])


def kernel(
    owners_ref, data_ref, tmpl_ref, out_ref,
    arch0, arch1, arch2, normed, columns, lhs0, lhs1, base, inv, band, win0, win1, part,
    y_out, y_in, xo, xi, yb_out, yb_in,
    g_send, g_recv, y_send, y_recv, x_send, x_recv,
):
    tm = lax.axis_index("tmpl")
    ch = lax.axis_index("chan")
    z, yh, core = tm // 4, lax.rem(tm // 2, 2), lax.rem(tm, 2)
    yl, x = ch // 4, lax.rem(ch, 4)
    e = 1 - 2 * core

    def block(dz, dyh):
        return lax.rem(z + 4 + dz * e, 4) * 4 + lax.rem(yh + dyh, 2) * 2 + core

    def holder(dz, dyh, dcore):
        near = lax.rem(z + dz, 4) * 4 + lax.rem(yh + dyh, 2) * 2 + lax.rem(core + dcore, 2)
        return {"tmpl": near, "chan": ch}

    def chan_at(dyl, dx):
        return lax.rem(yl + dyl, 2) * 4 + lax.rem(x + dx, 4)

    ahead = {"tmpl": block(1, 0), "chan": ch}
    behind = {"tmpl": block(-1, 0), "chan": ch}
    across = {"tmpl": block(0, 1), "chan": ch}
    mate = holder(0, 0, 1)
    x_dev = {-1: {"tmpl": tm, "chan": chan_at(0, 3)}, 1: {"tmpl": tm, "chan": chan_at(0, 1)}}
    y_dev = {"tmpl": tm, "chan": chan_at(1, 0)}

    barrier = pltpu.get_barrier_semaphore()
    chips = [(dz, dyh) for dyh in range(2) for dz in (2, 1, 3, 0) if dz or dyh]
    others = [holder(dz, dyh, dcore) for dcore in range(2) for dz, dyh in chips] + [mate]
    peers = others + [y_dev, x_dev[-1], x_dev[1]]
    for peer in peers:
        pl.semaphore_signal(barrier, inc=1, device_id=peer, device_id_type=MESH)
    pl.semaphore_wait(barrier, len(peers))

    def remote(src, dst, send, recv, device):
        return pltpu.make_async_remote_copy(
            src, dst, send, recv, device_id=device, device_id_type=MESH)

    archs = (arch0, arch1, arch2)
    first = (1 - yl) * 4 + lax.rem(x + 2, 4)
    starts = [
        pl.multiple_of(first * NS, NS),
        pl.multiple_of((1 - yl) * 1024, 1024),
        pl.multiple_of(yl * 1024, 1024),
    ]
    tree_targets = (ahead, behind, across, ahead, ahead, behind, ahead, mate) + (mate,) * 7
    carried = (None, None, None, (-1, 0), (0, 1), (0, 1), (-1, 1), None)
    carried += ((-1, 0), (1, 0), (0, 1), (-2, 0), (-1, 1), (1, 1), (-2, 1))

    def g_copy(g, m):
        mode = MODES[g]
        source = None
        if mode == "all":
            target = others[m]
        elif mode == "chip":
            target = others[m] if m < 7 else mate
            if m > 7:
                dz, dyh = chips[m - 8]
                source = holder((4 - dz) % 4, dyh, 0)["tmpl"]
        else:
            target = tree_targets[m]
            if carried[m] is not None:
                source = block(*carried[m])
        if source is None:
            src = data_ref.at[:, pl.ds(starts[g], GROUPS[g])]
            dst = archs[g].at[tm]
        else:
            src = dst = archs[g].at[source]
        return remote(src, dst, g_send.at[g, m], g_recv.at[g, m], target)

    def g_start(g):
        first = {"all": range(15), "chip": range(8), "tree": (2, 0, 1, 7)}[MODES[g]]
        for m in first:
            g_copy(g, m).start()
        archs[g][tm] = data_ref[:, pl.ds(starts[g], GROUPS[g])]

    def g_pass(g, m, on):
        g_copy(g, m).wait_recv()
        for k in on:
            g_copy(g, k).start()

    def g_stage1(g):
        if MODES[g] == "tree":
            g_pass(g, 0, (3, 8))
            g_pass(g, 1, (9,))
            g_pass(g, 2, (4, 5, 10))
        if MODES[g] == "chip":
            for m in (6, 1, 2, 0, 4, 5, 3):
                g_pass(g, m, (8 + m,))

    def g_stage2(g):
        if MODES[g] == "tree":
            g_pass(g, 3, (11,))
            g_pass(g, 4, (6, 12))
            g_pass(g, 5, (13,))

    def g_stage3(g):
        if MODES[g] == "tree":
            g_pass(g, 6, (14,))

    def g_finish(g):
        for m in range(0 if MODES[g] == "all" else 7, 15):
            g_copy(g, m).wait_recv()
        width = GROUPS[g]
        for b in range(NB):
            seg = archs[g][owners_ref[b]].astype(F32)
            seg = jnp.concatenate([seg, jnp.zeros((4, width), F32)], axis=0)
            small = seg * (1.0 / 256)
            power = jnp.minimum(small * small, 2.0**120)
            high = power.astype(BF16)
            low = (power - high.astype(F32)).astype(BF16)
            squares = jnp.concatenate([high, low], axis=0)
            for n in range(width // NS - 1):
                energy = jnp.dot(squares[:, n * NS : n * NS + 512], band[...],
                                 preferred_element_type=F32)
                mean = (energy[:16] + energy[16:]) * (65536.0 / W)
                scale = 1.0 / (jnp.sqrt(mean + EPS) * math.sqrt(W))
                for q in range(CG):
                    for s in range(4):
                        inv[b * CG + q, 4 * s : 4 * s + 4, pl.ds(starts[g] + n * NS, NS)] = (
                            scale[4 * q : 4 * q + 4])
            seg = seg.astype(BF16)
            for s in range(4):
                turned = pltpu.roll(seg, width - s, 1) if s else seg
                turned = turned.astype(F32)
                for q in range(CG):
                    base[b * CG + q, 4 * s : 4 * s + 4, pl.ds(starts[g], width)] = (
                        turned[4 * q : 4 * q + 4])

    g_start(0)
    g_start(1)
    g_start(2)

    sample = lax.broadcasted_iota(jnp.int32, (512, NS), 0)
    lag_of = lax.broadcasted_iota(jnp.int32, (512, NS), 1)
    inside = jnp.logical_and(sample >= lag_of, sample < lag_of + W)
    band[...] = jnp.where(inside, 1.0, 0.0).astype(BF16)

    for c in range(C):
        values = tmpl_ref[c].astype(F32)
        power = jnp.sum(values * values, axis=0, keepdims=True) * (1.0 / W)
        scaled = values * (1.0 / (jnp.sqrt(power + EPS) * math.sqrt(W)))
        for j in range(2):
            normed[j] = scaled[:, j * 128 : j * 128 + 128]
            for s in range(4):
                row = c // 4 * 16 + 4 * s + c % 4
                columns[j, pl.ds(row, W // 4, stride=KR), :] = (
                    normed[j, pl.ds(s, W // 4, stride=4), :])
    for lhs, (lo, hi) in ((lhs0, PHASES[0]), (lhs1, PHASES[1])):
        tail = min(hi + 32, W // 4)
        for j in range(2):
            band_rows = slice(j * 128, j * 128 + 128)
            cut = (hi - lo) * KR
            lhs[band_rows, :cut] = columns[j, lo * KR : hi * KR, :].T.astype(BF16)
            lhs[band_rows, cut:] = columns[j, (lo + 32) * KR : tail * KR, :].T.astype(BF16)

    g_stage1(0)
    g_stage2(0)
    g_stage3(0)
    g_finish(0)

    def y_copy(n):
        return remote(y_out.at[n], y_in.at[n], y_send.at[n], y_recv.at[n], y_dev)

    def yb_copy():
        return remote(yb_out, yb_in, y_send.at[4], y_recv.at[4], y_dev)

    def x_span(t, half):
        return AH[half] if t == 2 else BH[half]

    def x_slot(t):
        return t % 2

    def x_copy(t, kind, half):
        span = rows(x_span(t, half))
        direction = -1 if half == 0 else 1
        if kind == 2:
            direction = -direction
        n = (t * 3 + kind) * 2 + half
        return remote(
            xo.at[x_slot(t), kind, span], xi.at[x_slot(t), kind, span],
            x_send.at[n], x_recv.at[n], x_dev[direction])

    def x_put(t, kind, half, value):
        xo[x_slot(t), kind, rows(x_span(t, half))] = value.astype(BF16)
        x_copy(t, kind, half).start()

    def x_got(t, kind, half):
        x_copy(t, kind, half).wait_recv()
        return xi[x_slot(t), kind, rows(x_span(t, half))].astype(F32)

    def own(n, span):
        return part[n, rows(span)]

    def local(t, n, half):
        span = x_span(t, half)
        if t == 2:
            return own(n, span) + y_in[n - 4, rows(span)].astype(F32)
        return own(n, span)

    def send_far(t, n):
        for half in (0, 1):
            x_put(t, 0, half, local(t, n, half))

    def send_direct(t, n, half):
        x_put(t, 2, half, local(t, n, half))

    def send_relay(t, n, half):
        x_put(t, 1, half, local(t, n, half) + x_got(t, 0, half))

    def total(t, n, half):
        return local(t, n, half) + x_got(t, 1, half) + x_got(t, 2, half)

    def y_first(n):
        y_out[n] = own(n, A).astype(BF16)
        y_copy(n).start()

    def between_1():
        g_stage2(2)

    def between_2():
        g_stage3(2)

    def between_3():
        g_finish(2)

    def after_0():
        y_first(0)
        send_far(0, 0)

    def after_1():
        y_first(1)
        send_direct(0, 1, 0)

    def after_2():
        y_first(2)
        send_direct(0, 2, 1)

    def after_3():
        y_first(3)

    def after_4():
        send_far(1, 4)
        send_relay(0, 1, 1)
        send_relay(0, 2, 0)

    def after_5():
        send_direct(1, 5, 0)
        y_copy(0).wait_recv()
        send_far(2, 4)

    def after_6():
        send_direct(1, 6, 1)

    betweens = [between_1, between_2, between_3]
    actions = [after_1, after_2, after_3, after_4, after_5, after_6]

    def dest(n):
        step = lax.rem(n, 4)
        dx = jnp.where(step == 0, 2, jnp.where(step == 1, 1, jnp.where(step == 2, 3, 0)))
        return lax.rem(yl + 1 + n // 4, 2) * 4 + lax.rem(x + dx, 4)

    def build(win, half, n):
        lag = pl.multiple_of(dest(n) * NS, NS)
        taps = TAPS[half]
        for b in range(NB):
            cols = slice(b * NS, (b + 1) * NS)
            for q in range(CG):
                wide = base[b * CG + q, :, pl.ds(lag, 512)].astype(BF16)
                scale = inv[b * CG + q, :, pl.ds(lag, NS)]
                for p in range(*PHASES[half]):
                    turned = pltpu.roll(wide, 512 - 4 * p, 1) if p else wide
                    turned = turned.astype(F32)
                    row = taps.index(p) * KR + q * 16
                    win[row : row + 16, cols] = (turned[:, :NS] * scale).astype(BF16)
                    if p + 32 in taps:
                        row = taps.index(p + 32) * KR + q * 16
                        win[row : row + 16, cols] = (
                            turned[:, 128 : 128 + NS] * scale).astype(BF16)

    build(win0, 0, 0)
    build(win1, 1, 0)
    part[0] = jnp.dot(lhs0[...], win0[...], preferred_element_type=F32)
    g_stage1(1)
    part[0] += jnp.dot(lhs1[...], win1[...], preferred_element_type=F32)
    after_0()
    g_stage1(2)
    g_finish(1)
    build(win0, 0, 1)

    def chunk(n, carry):
        build(win1, 1, n)
        part[n] = jnp.dot(lhs0[...], win0[...], preferred_element_type=F32)
        for m, action in enumerate(betweens):
            pl.when(n == m + 1)(action)
        build(win0, 0, jnp.minimum(n + 1, 7))
        part[n] += jnp.dot(lhs1[...], win1[...], preferred_element_type=F32)
        for m, action in enumerate(actions):
            pl.when(n == m + 1)(action)
        return carry

    lax.fori_loop(1, 8, chunk, 0)

    send_relay(1, 5, 1)
    send_relay(1, 6, 0)
    y_copy(1).wait_recv()
    send_direct(2, 5, 0)
    send_relay(2, 5, 1)
    for half in (0, 1):
        yb_out[rows(x_span(0, half), B[0])] = total(0, 3, half).astype(BF16)
    yb_copy().start()
    y_copy(2).wait_recv()
    send_direct(2, 6, 1)
    send_relay(2, 6, 0)

    def finish(span, value):
        for b in range(NB):
            out_ref[b, rows(span)] = value[:, b * NS : (b + 1) * NS]

    y_copy(3).wait_recv()
    for half in (0, 1):
        finish(AH[half], total(2, 7, half))
    yb_copy().wait_recv()
    for half in (0, 1):
        span = x_span(1, half)
        finish(span, total(1, 7, half) + yb_in[rows(span, B[0])].astype(F32))

    for g in range(3):
        for m in range(15):
            g_copy(g, m).wait_send()
    for n in range(4):
        y_copy(n).wait_send()
    yb_copy().wait_send()
    for t in range(3):
        for kind in range(3):
            for half in (0, 1):
                x_copy(t, kind, half).wait_send()


def body(data, templates, counts, owners):
    vmem = pl.BlockSpec(memory_space=pltpu.VMEM)
    dma = pltpu.SemaphoreType.DMA
    traces = pl.pallas_call(
        kernel,
        out_shape=jax.ShapeDtypeStruct((NB, K, NS), F32),
        in_specs=[pl.BlockSpec(memory_space=pltpu.SMEM), vmem, vmem],
        out_specs=vmem,
        scratch_shapes=[
            pltpu.VMEM((16, C, GROUPS[0]), BF16),
            pltpu.VMEM((16, C, GROUPS[1]), BF16),
            pltpu.VMEM((16, C, GROUPS[2]), BF16),
            pltpu.VMEM((2, W, 128), F32),
            pltpu.VMEM((2, W * C, 128), F32),
            pltpu.VMEM((K, KH[0]), BF16),
            pltpu.VMEM((K, KH[1]), BF16),
            pltpu.VMEM((NB * CG, 16, LB), F32),
            pltpu.VMEM((NB * CG, 16, LO), F32),
            pltpu.VMEM((512, NS), BF16),
            pltpu.VMEM((KH[0], NC), BF16),
            pltpu.VMEM((KH[1], NC), BF16),
            pltpu.VMEM((8, K, NC), F32),
            pltpu.VMEM((4, A[1], NC), BF16),
            pltpu.VMEM((4, A[1], NC), BF16),
            pltpu.VMEM((2, 3, K, NC), BF16),
            pltpu.VMEM((2, 3, K, NC), BF16),
            pltpu.VMEM((B[1] - B[0], NC), BF16),
            pltpu.VMEM((B[1] - B[0], NC), BF16),
            dma((3, 15)), dma((3, 15)), dma((5,)), dma((5,)), dma((18,)), dma((18,)),
        ],
        compiler_params=pltpu.CompilerParams(
            collective_id=0, has_side_effects=True, vmem_limit_bytes=60 << 20),
    )(owners, data[0], jnp.transpose(templates, (1, 2, 0)))
    live = jnp.arange(K, dtype=jnp.int32) < counts[0]
    return jnp.transpose(jnp.where(live[None, :, None], traces, 0.0), (1, 0, 2))


def solution(mesh):
    placed = (P("tmpl", "chan", None), P("tmpl", "chan", None), P("tmpl"), P())
    return jax.shard_map(
        body, mesh=mesh, in_specs=placed, out_specs=P("tmpl", None, "chan"), check_vma=False
    )
```

```python
import math

import jax
import jax.numpy as jnp
from jax import lax
from jax.experimental import pallas as pl
from jax.experimental.pallas import tpu as pltpu
from jax.sharding import PartitionSpec as P

W = 200
NB = 3
LO = 2048
C = 12
CG = C // 4
LB = 2304
K = 256
KR = 16 * CG
PHASES = ((0, 16), (16, 32))
TAPS = tuple(tuple(g for lo in (a, a + 32) for g in range(lo, lo + 16) if 4 * g < W) for a, _ in PHASES)
KH = tuple(len(taps) * KR for taps in TAPS)
NS = 256
NC = NB * NS
EPS = 1e-06
MESH = pl.DeviceIdType.MESH
GROUPS = (512, 1280, 1280)
MODES = ("chip", "chip", "tree")

A = (0, 112)
AH = ((0, 64), (64, 112))
B = (112, 256)
BH = ((192, 256), (112, 192))
F32 = jnp.float32
BF16 = jnp.bfloat16


def rows(span, base=0):
    return pl.ds(span[0] - base, span[1] - span[0])


def kernel(
    owners_ref, data_ref, tmpl_ref, out_ref,
    arch0, arch1, arch2, normed, columns, lhs0, lhs1, base, inv, band, win0, win1, part,
    y_out, y_in, xo, xi, yb_out, yb_in,
    g_send, g_recv, y_send, y_recv, x_send, x_recv,
):
    tm = lax.axis_index("tmpl")
    ch = lax.axis_index("chan")
    z, yh, core = tm // 4, lax.rem(tm // 2, 2), lax.rem(tm, 2)
    yl, x = ch // 4, lax.rem(ch, 4)
    e = 1 - 2 * core

    def block(dz, dyh):
        return lax.rem(z + 4 + dz * e, 4) * 4 + lax.rem(yh + dyh, 2) * 2 + core

    def holder(dz, dyh, dcore):
        near = lax.rem(z + dz, 4) * 4 + lax.rem(yh + dyh, 2) * 2 + lax.rem(core + dcore, 2)
        return {"tmpl": near, "chan": ch}

    def chan_at(dyl, dx):
        return lax.rem(yl + dyl, 2) * 4 + lax.rem(x + dx, 4)

    ahead = {"tmpl": block(1, 0), "chan": ch}
    behind = {"tmpl": block(-1, 0), "chan": ch}
    across = {"tmpl": block(0, 1), "chan": ch}
    mate = holder(0, 0, 1)
    x_dev = {-1: {"tmpl": tm, "chan": chan_at(0, 3)}, 1: {"tmpl": tm, "chan": chan_at(0, 1)}}
    y_dev = {"tmpl": tm, "chan": chan_at(1, 0)}

    barrier = pltpu.get_barrier_semaphore()
    chips = [(dz, dyh) for dyh in range(2) for dz in (2, 1, 3, 0) if dz or dyh]
    others = [holder(dz, dyh, dcore) for dcore in range(2) for dz, dyh in chips] + [mate]
    peers = others[:7] + [mate, y_dev, x_dev[-1], x_dev[1]]
    for peer in peers:
        pl.semaphore_signal(barrier, inc=1, device_id=peer, device_id_type=MESH)
    pl.semaphore_wait(barrier, len(peers))

    def remote(src, dst, send, recv, device):
        return pltpu.make_async_remote_copy(
            src, dst, send, recv, device_id=device, device_id_type=MESH)

    archs = (arch0, arch1, arch2)
    first = (1 - yl) * 4 + lax.rem(x + 2, 4)
    starts = [
        pl.multiple_of(first * NS, NS),
        pl.multiple_of((1 - yl) * 1024, 1024),
        pl.multiple_of(yl * 1024, 1024),
    ]
    tree_targets = (ahead, behind, across, ahead, ahead, behind, ahead, mate) + (mate,) * 7
    carried = (None, None, None, (-1, 0), (0, 1), (0, 1), (-1, 1), None)
    carried += ((-1, 0), (1, 0), (0, 1), (-2, 0), (-1, 1), (1, 1), (-2, 1))

    def g_copy(g, m):
        mode = MODES[g]
        source = None
        if mode == "all":
            target = others[m]
        elif mode == "chip":
            target = others[m] if m < 7 else mate
            if m > 7:
                dz, dyh = chips[m - 8]
                source = holder((4 - dz) % 4, dyh, 0)["tmpl"]
        else:
            target = tree_targets[m]
            if carried[m] is not None:
                source = block(*carried[m])
        if source is None:
            src = data_ref.at[:, pl.ds(starts[g], GROUPS[g])]
            dst = archs[g].at[tm]
        else:
            src = dst = archs[g].at[source]
        return remote(src, dst, g_send.at[g, m], g_recv.at[g, m], target)

    def g_start(g):
        first = {"all": range(15), "chip": range(8), "tree": (2, 0, 1, 7)}[MODES[g]]
        for m in first:
            g_copy(g, m).start()
        archs[g][tm] = data_ref[:, pl.ds(starts[g], GROUPS[g])]

    def g_pass(g, m, on):
        g_copy(g, m).wait_recv()
        for k in on:
            g_copy(g, k).start()

    def g_stage1(g):
        if MODES[g] == "tree":
            g_pass(g, 0, (3, 8))
            g_pass(g, 1, (9,))
            g_pass(g, 2, (4, 5, 10))
        if MODES[g] == "chip":
            for m in (6, 1, 2, 0, 4, 5, 3):
                g_pass(g, m, (8 + m,))

    def g_stage2(g):
        if MODES[g] == "tree":
            g_pass(g, 3, (11,))
            g_pass(g, 4, (6, 12))
            g_pass(g, 5, (13,))

    def g_stage3(g):
        if MODES[g] == "tree":
            g_pass(g, 6, (14,))

    def g_finish(g):
        for m in range(0 if MODES[g] == "all" else 7, 15):
            g_copy(g, m).wait_recv()
        width = GROUPS[g]
        for b in range(NB):
            seg = archs[g][owners_ref[b]].astype(F32)
            seg = jnp.concatenate([seg, jnp.zeros((4, width), F32)], axis=0)
            small = seg * (1.0 / 256)
            power = jnp.minimum(small * small, 2.0**120)
            high = power.astype(BF16)
            low = (power - high.astype(F32)).astype(BF16)
            squares = jnp.concatenate([high, low], axis=0)
            for n in range(width // NS - 1):
                energy = jnp.dot(squares[:, n * NS : n * NS + 512], band[...],
                                 preferred_element_type=F32)
                mean = (energy[:16] + energy[16:]) * (65536.0 / W)
                scale = 1.0 / (jnp.sqrt(mean + EPS) * math.sqrt(W))
                for q in range(CG):
                    for s in range(4):
                        inv[b * CG + q, 4 * s : 4 * s + 4, pl.ds(starts[g] + n * NS, NS)] = (
                            scale[4 * q : 4 * q + 4])
            seg = seg.astype(BF16)
            for s in range(4):
                turned = pltpu.roll(seg, width - s, 1) if s else seg
                turned = turned.astype(F32)
                for q in range(CG):
                    base[b * CG + q, 4 * s : 4 * s + 4, pl.ds(starts[g], width)] = (
                        turned[4 * q : 4 * q + 4])

    g_start(0)
    g_start(2)
    g_start(1)

    sample = lax.broadcasted_iota(jnp.int32, (512, NS), 0)
    lag_of = lax.broadcasted_iota(jnp.int32, (512, NS), 1)
    inside = jnp.logical_and(sample >= lag_of, sample < lag_of + W)
    band[...] = jnp.where(inside, 1.0, 0.0).astype(BF16)

    for c in range(C):
        values = tmpl_ref[c].astype(F32)
        power = jnp.sum(values * values, axis=0, keepdims=True) * (1.0 / W)
        scaled = values * (1.0 / (jnp.sqrt(power + EPS) * math.sqrt(W)))
        for j in range(2):
            normed[j] = scaled[:, j * 128 : j * 128 + 128]
            for s in range(4):
                row = c // 4 * 16 + 4 * s + c % 4
                columns[j, pl.ds(row, W // 4, stride=KR), :] = (
                    normed[j, pl.ds(s, W // 4, stride=4), :])
    for lhs, (lo, hi) in ((lhs0, PHASES[0]), (lhs1, PHASES[1])):
        tail = min(hi + 32, W // 4)
        for j in range(2):
            band_rows = slice(j * 128, j * 128 + 128)
            cut = (hi - lo) * KR
            lhs[band_rows, :cut] = columns[j, lo * KR : hi * KR, :].T.astype(BF16)
            lhs[band_rows, cut:] = columns[j, (lo + 32) * KR : tail * KR, :].T.astype(BF16)

    g_stage1(0)
    g_stage2(0)
    g_stage3(0)
    g_finish(0)

    def y_copy(n):
        return remote(y_out.at[n], y_in.at[n], y_send.at[n], y_recv.at[n], y_dev)

    def yb_copy():
        return remote(yb_out, yb_in, y_send.at[4], y_recv.at[4], y_dev)

    def x_span(t, half):
        return AH[half] if t == 2 else BH[half]

    def x_slot(t):
        return t % 2

    def x_copy(t, kind, half):
        span = rows(x_span(t, half))
        direction = -1 if half == 0 else 1
        if kind == 2:
            direction = -direction
        n = (t * 3 + kind) * 2 + half
        return remote(
            xo.at[x_slot(t), kind, span], xi.at[x_slot(t), kind, span],
            x_send.at[n], x_recv.at[n], x_dev[direction])

    def x_put(t, kind, half, value):
        xo[x_slot(t), kind, rows(x_span(t, half))] = value.astype(BF16)
        x_copy(t, kind, half).start()

    def x_got(t, kind, half):
        x_copy(t, kind, half).wait_recv()
        return xi[x_slot(t), kind, rows(x_span(t, half))].astype(F32)

    def own(n, span):
        return part[n, rows(span)]

    def local(t, n, half):
        span = x_span(t, half)
        if t == 2:
            return own(n, span) + y_in[n - 4, rows(span)].astype(F32)
        return own(n, span)

    def send_far(t, n):
        for half in (0, 1):
            x_put(t, 0, half, local(t, n, half))

    def send_direct(t, n, half):
        x_put(t, 2, half, local(t, n, half))

    def send_relay(t, n, half):
        x_put(t, 1, half, local(t, n, half) + x_got(t, 0, half))

    def total(t, n, half):
        return local(t, n, half) + x_got(t, 1, half) + x_got(t, 2, half)

    def y_first(n):
        y_out[n] = own(n, A).astype(BF16)
        y_copy(n).start()

    def between_1():
        g_stage2(2)

    def between_2():
        g_stage3(2)

    def between_3():
        g_finish(2)

    def after_0():
        y_first(0)
        send_far(0, 0)

    def after_1():
        y_first(1)
        send_direct(0, 1, 0)

    def after_2():
        y_first(2)
        send_direct(0, 2, 1)
        send_relay(0, 1, 1)
        send_relay(0, 2, 0)

    def after_3():
        y_first(3)

    def after_4():
        send_far(1, 4)
        y_copy(0).wait_recv()
        send_far(2, 4)

    def after_5():
        send_direct(1, 5, 0)
        y_copy(1).wait_recv()
        send_direct(2, 5, 0)

    def after_6():
        send_direct(1, 6, 1)
        for half in (0, 1):
            yb_out[rows(x_span(0, half), B[0])] = total(0, 3, half).astype(BF16)
        yb_copy().start()

    betweens = [between_1, between_2, between_3]
    actions = [after_1, after_2, after_3, after_4, after_5, after_6]

    def dest(n):
        step = lax.rem(n, 4)
        dx = jnp.where(step == 0, 2, jnp.where(step == 1, 1, jnp.where(step == 2, 3, 0)))
        return lax.rem(yl + 1 + n // 4, 2) * 4 + lax.rem(x + dx, 4)

    def build(win, half, n):
        lag = pl.multiple_of(dest(n) * NS, NS)
        taps = TAPS[half]
        for b in range(NB):
            cols = slice(b * NS, (b + 1) * NS)
            for q in range(CG):
                wide = base[b * CG + q, :, pl.ds(lag, 512)].astype(BF16)
                scale = inv[b * CG + q, :, pl.ds(lag, NS)]
                for p in range(*PHASES[half]):
                    turned = pltpu.roll(wide, 512 - 4 * p, 1) if p else wide
                    turned = turned.astype(F32)
                    row = taps.index(p) * KR + q * 16
                    win[row : row + 16, cols] = (turned[:, :NS] * scale).astype(BF16)
                    if p + 32 in taps:
                        row = taps.index(p + 32) * KR + q * 16
                        win[row : row + 16, cols] = (
                            turned[:, 128 : 128 + NS] * scale).astype(BF16)

    build(win0, 0, 0)
    build(win1, 1, 0)
    part[0] = jnp.dot(lhs0[...], win0[...], preferred_element_type=F32)
    g_stage1(1)
    g_stage1(2)
    part[0] += jnp.dot(lhs1[...], win1[...], preferred_element_type=F32)
    after_0()
    g_finish(1)
    build(win0, 0, 1)

    def chunk(n, carry):
        build(win1, 1, n)
        part[n] = jnp.dot(lhs0[...], win0[...], preferred_element_type=F32)
        for m, action in enumerate(betweens):
            pl.when(n == m + 1)(action)
        build(win0, 0, jnp.minimum(n + 1, 7))
        part[n] += jnp.dot(lhs1[...], win1[...], preferred_element_type=F32)
        for m, action in enumerate(actions):
            pl.when(n == m + 1)(action)
        return carry

    lax.fori_loop(1, 8, chunk, 0)

    send_relay(1, 5, 1)
    send_relay(1, 6, 0)
    y_copy(2).wait_recv()
    send_direct(2, 6, 1)
    send_relay(2, 5, 1)
    send_relay(2, 6, 0)

    def finish(span, value):
        for b in range(NB):
            out_ref[b, rows(span)] = value[:, b * NS : (b + 1) * NS]

    y_copy(3).wait_recv()
    for half in (0, 1):
        finish(AH[half], total(2, 7, half))
    yb_copy().wait_recv()
    for half in (0, 1):
        span = x_span(1, half)
        finish(span, total(1, 7, half) + yb_in[rows(span, B[0])].astype(F32))

    for g in range(3):
        for m in range(15):
            g_copy(g, m).wait_send()
    for n in range(4):
        y_copy(n).wait_send()
    yb_copy().wait_send()
    for t in range(3):
        for kind in range(3):
            for half in (0, 1):
                x_copy(t, kind, half).wait_send()


def body(data, templates, counts, owners):
    vmem = pl.BlockSpec(memory_space=pltpu.VMEM)
    dma = pltpu.SemaphoreType.DMA
    traces = pl.pallas_call(
        kernel,
        out_shape=jax.ShapeDtypeStruct((NB, K, NS), F32),
        in_specs=[pl.BlockSpec(memory_space=pltpu.SMEM), vmem, vmem],
        out_specs=vmem,
        scratch_shapes=[
            pltpu.VMEM((16, C, GROUPS[0]), BF16),
            pltpu.VMEM((16, C, GROUPS[1]), BF16),
            pltpu.VMEM((16, C, GROUPS[2]), BF16),
            pltpu.VMEM((2, W, 128), F32),
            pltpu.VMEM((2, W * C, 128), F32),
            pltpu.VMEM((K, KH[0]), BF16),
            pltpu.VMEM((K, KH[1]), BF16),
            pltpu.VMEM((NB * CG, 16, LB), F32),
            pltpu.VMEM((NB * CG, 16, LO), F32),
            pltpu.VMEM((512, NS), BF16),
            pltpu.VMEM((KH[0], NC), BF16),
            pltpu.VMEM((KH[1], NC), BF16),
            pltpu.VMEM((8, K, NC), F32),
            pltpu.VMEM((4, A[1], NC), BF16),
            pltpu.VMEM((4, A[1], NC), BF16),
            pltpu.VMEM((2, 3, K, NC), BF16),
            pltpu.VMEM((2, 3, K, NC), BF16),
            pltpu.VMEM((B[1] - B[0], NC), BF16),
            pltpu.VMEM((B[1] - B[0], NC), BF16),
            dma((3, 15)), dma((3, 15)), dma((5,)), dma((5,)), dma((18,)), dma((18,)),
        ],
        compiler_params=pltpu.CompilerParams(
            collective_id=0, has_side_effects=True, vmem_limit_bytes=60 << 20),
    )(owners, data[0], jnp.transpose(templates, (1, 2, 0)))
    live = jnp.arange(K, dtype=jnp.int32) < counts[0]
    return jnp.transpose(jnp.where(live[None, :, None], traces, 0.0), (1, 0, 2))


def solution(mesh):
    placed = (P("tmpl", "chan", None), P("tmpl", "chan", None), P("tmpl"), P())
    return jax.shard_map(
        body, mesh=mesh, in_specs=placed, out_specs=P("tmpl", None, "chan"), check_vma=False
    )
```

```python
import math

import jax
import jax.numpy as jnp
from jax import lax
from jax.experimental import pallas as pl
from jax.experimental.pallas import tpu as pltpu
from jax.sharding import PartitionSpec as P

W = 200
NB = 3
LO = 2048
C = 12
CG = C // 4
LB = 2304
K = 256
KR = 16 * CG
PHASES = ((0, 16), (16, 32))
TAPS = tuple(tuple(g for lo in (a, a + 32) for g in range(lo, lo + 16) if 4 * g < W) for a, _ in PHASES)
KH = tuple(len(taps) * KR for taps in TAPS)
NS = 256
NC = NB * NS
EPS = 1e-06
MESH = pl.DeviceIdType.MESH
GROUPS = (512, 1280, 1280)
MODES = ("chip", "chip", "tree")

A = (0, 112)
AH = ((0, 64), (64, 112))
B = (112, 256)
BH = ((192, 256), (112, 192))
F32 = jnp.float32
BF16 = jnp.bfloat16


def rows(span, base=0):
    return pl.ds(span[0] - base, span[1] - span[0])


def kernel(
    owners_ref, data_ref, tmpl_ref, out_ref,
    arch0, arch1, arch2, normed, columns, lhs0, lhs1, base, inv, band, win0, win1, part,
    y_out, y_in, xo, xi, yb_out, yb_in, held, held_sem,
    g_send, g_recv, y_send, y_recv, x_send, x_recv,
):
    tm = lax.axis_index("tmpl")
    ch = lax.axis_index("chan")
    z, yh, core = tm // 4, lax.rem(tm // 2, 2), lax.rem(tm, 2)
    yl, x = ch // 4, lax.rem(ch, 4)
    e = 1 - 2 * core

    def block(dz, dyh):
        return lax.rem(z + 4 + dz * e, 4) * 4 + lax.rem(yh + dyh, 2) * 2 + core

    def holder(dz, dyh, dcore):
        near = lax.rem(z + dz, 4) * 4 + lax.rem(yh + dyh, 2) * 2 + lax.rem(core + dcore, 2)
        return {"tmpl": near, "chan": ch}

    def chan_at(dyl, dx):
        return lax.rem(yl + dyl, 2) * 4 + lax.rem(x + dx, 4)

    ahead = {"tmpl": block(1, 0), "chan": ch}
    behind = {"tmpl": block(-1, 0), "chan": ch}
    across = {"tmpl": block(0, 1), "chan": ch}
    mate = holder(0, 0, 1)
    x_dev = {-1: {"tmpl": tm, "chan": chan_at(0, 3)}, 1: {"tmpl": tm, "chan": chan_at(0, 1)}}
    y_dev = {"tmpl": tm, "chan": chan_at(1, 0)}

    fetch = pltpu.make_async_copy(tmpl_ref, held.at[pl.ds(0, C)], held_sem)
    fetch.start()
    barrier = pltpu.get_barrier_semaphore()
    chips = [(dz, dyh) for dyh in range(2) for dz in (2, 1, 3, 0) if dz or dyh]
    others = [holder(dz, dyh, dcore) for dcore in range(2) for dz, dyh in chips] + [mate]
    peers = others[:7] + [mate, y_dev, x_dev[-1], x_dev[1]]
    for peer in peers:
        pl.semaphore_signal(barrier, inc=1, device_id=peer, device_id_type=MESH)
    pl.semaphore_wait(barrier, len(peers))

    def remote(src, dst, send, recv, device):
        return pltpu.make_async_remote_copy(
            src, dst, send, recv, device_id=device, device_id_type=MESH)

    archs = (arch0, arch1, arch2)
    first = (1 - yl) * 4 + lax.rem(x + 2, 4)
    starts = [
        pl.multiple_of(first * NS, NS),
        pl.multiple_of((1 - yl) * 1024, 1024),
        pl.multiple_of(yl * 1024, 1024),
    ]
    tree_targets = (ahead, behind, across, ahead, ahead, behind, ahead, mate) + (mate,) * 7
    carried = (None, None, None, (-1, 0), (0, 1), (0, 1), (-1, 1), None)
    carried += ((-1, 0), (1, 0), (0, 1), (-2, 0), (-1, 1), (1, 1), (-2, 1))

    def g_copy(g, m):
        mode = MODES[g]
        source = None
        if mode == "all":
            target = others[m]
        elif mode == "chip":
            target = others[m] if m < 7 else mate
            if m > 7:
                dz, dyh = chips[m - 8]
                source = holder((4 - dz) % 4, dyh, 0)["tmpl"]
        else:
            target = tree_targets[m]
            if carried[m] is not None:
                source = block(*carried[m])
        if source is None:
            src = data_ref.at[:, pl.ds(starts[g], GROUPS[g])]
            dst = archs[g].at[tm]
        else:
            src = dst = archs[g].at[source]
        return remote(src, dst, g_send.at[g, m], g_recv.at[g, m], target)

    def g_start(g):
        first = {"all": range(15), "chip": range(8), "tree": (2, 0, 1, 7)}[MODES[g]]
        for m in first:
            g_copy(g, m).start()
        archs[g][tm] = data_ref[:, pl.ds(starts[g], GROUPS[g])]

    def g_pass(g, m, on):
        g_copy(g, m).wait_recv()
        for k in on:
            g_copy(g, k).start()

    def g_stage1(g):
        if MODES[g] == "tree":
            g_pass(g, 0, (3, 8))
            g_pass(g, 1, (9,))
            g_pass(g, 2, (4, 5, 10))
        if MODES[g] == "chip":
            for m in (6, 1, 2, 0, 4, 5, 3):
                g_pass(g, m, (8 + m,))

    def g_stage2(g):
        if MODES[g] == "tree":
            g_pass(g, 3, (11,))
            g_pass(g, 4, (6, 12))
            g_pass(g, 5, (13,))

    def g_stage3(g):
        if MODES[g] == "tree":
            g_pass(g, 6, (14,))

    def g_finish(g):
        for m in range(0 if MODES[g] == "all" else 7, 15):
            g_copy(g, m).wait_recv()
        width = GROUPS[g]
        for b in range(NB):
            seg = archs[g][owners_ref[b]].astype(F32)
            seg = jnp.concatenate([seg, jnp.zeros((4, width), F32)], axis=0)
            small = seg * (1.0 / 256)
            power = jnp.minimum(small * small, 2.0**120)
            high = power.astype(BF16)
            low = (power - high.astype(F32)).astype(BF16)
            squares = jnp.concatenate([high, low], axis=0)
            for n in range(width // NS - 1):
                energy = jnp.dot(squares[:, n * NS : n * NS + 512], band[...],
                                 preferred_element_type=F32)
                mean = (energy[:16] + energy[16:]) * (65536.0 / W)
                scale = 1.0 / (jnp.sqrt(mean + EPS) * math.sqrt(W))
                for q in range(CG):
                    for s in range(4):
                        inv[b * CG + q, 4 * s : 4 * s + 4, pl.ds(starts[g] + n * NS, NS)] = (
                            scale[4 * q : 4 * q + 4])
            seg = seg.astype(BF16)
            for s in range(4):
                turned = pltpu.roll(seg, width - s, 1) if s else seg
                turned = turned.astype(F32)
                for q in range(CG):
                    base[b * CG + q, 4 * s : 4 * s + 4, pl.ds(starts[g], width)] = (
                        turned[4 * q : 4 * q + 4])

    g_start(0)
    g_start(2)
    g_start(1)

    sample = lax.broadcasted_iota(jnp.int32, (512, NS), 0)
    lag_of = lax.broadcasted_iota(jnp.int32, (512, NS), 1)
    inside = jnp.logical_and(sample >= lag_of, sample < lag_of + W)
    band[...] = jnp.where(inside, 1.0, 0.0).astype(BF16)

    fetch.wait()
    for c in range(C):
        values = held[c].astype(F32)
        power = jnp.sum(values * values, axis=0, keepdims=True) * (1.0 / W)
        scaled = values * (1.0 / (jnp.sqrt(power + EPS) * math.sqrt(W)))
        for j in range(2):
            normed[j, :W] = scaled[:, j * 128 : j * 128 + 128]
            for s in range(4):
                row = c // 4 * 16 + 4 * s + c % 4
                columns[j, pl.ds(row, W // 4, stride=KR), :] = (
                    normed[j, pl.ds(s, W // 4, stride=4), :])
    for lhs, (lo, hi) in ((lhs0, PHASES[0]), (lhs1, PHASES[1])):
        tail = min(hi + 32, W // 4)
        for j in range(2):
            band_rows = slice(j * 128, j * 128 + 128)
            cut = (hi - lo) * KR
            lhs[band_rows, :cut] = columns[j, lo * KR : hi * KR, :].T.astype(BF16)
            lhs[band_rows, cut:] = columns[j, (lo + 32) * KR : tail * KR, :].T.astype(BF16)

    g_stage1(0)
    g_stage2(0)
    g_stage3(0)
    g_finish(0)

    def y_copy(n):
        return remote(y_out.at[n], y_in.at[n], y_send.at[n], y_recv.at[n], y_dev)

    def yb_copy():
        return remote(yb_out, yb_in, y_send.at[4], y_recv.at[4], y_dev)

    def x_span(t, half):
        return AH[half] if t == 2 else BH[half]

    def x_slot(t):
        return t % 2

    def x_copy(t, kind, half):
        span = rows(x_span(t, half))
        direction = -1 if half == 0 else 1
        if kind == 2:
            direction = -direction
        n = (t * 3 + kind) * 2 + half
        return remote(
            xo.at[x_slot(t), kind, span], xi.at[x_slot(t), kind, span],
            x_send.at[n], x_recv.at[n], x_dev[direction])

    def x_put(t, kind, half, value):
        xo[x_slot(t), kind, rows(x_span(t, half))] = value.astype(BF16)
        x_copy(t, kind, half).start()

    def x_got(t, kind, half):
        x_copy(t, kind, half).wait_recv()
        return xi[x_slot(t), kind, rows(x_span(t, half))].astype(F32)

    def own(n, span):
        return part[n, rows(span)]

    def local(t, n, half):
        span = x_span(t, half)
        if t == 2:
            return own(n, span) + y_in[n - 4, rows(span)].astype(F32)
        return own(n, span)

    def send_far(t, n):
        for half in (0, 1):
            x_put(t, 0, half, local(t, n, half))

    def send_direct(t, n, half):
        x_put(t, 2, half, local(t, n, half))

    def send_relay(t, n, half):
        x_put(t, 1, half, local(t, n, half) + x_got(t, 0, half))

    def total(t, n, half):
        return local(t, n, half) + x_got(t, 1, half) + x_got(t, 2, half)

    def y_first(n):
        y_out[n] = own(n, A).astype(BF16)
        y_copy(n).start()

    def between_1():
        g_stage2(2)

    def between_2():
        g_stage3(2)

    def between_3():
        g_finish(2)

    def after_0():
        y_first(0)
        send_far(0, 0)

    def after_1():
        y_first(1)
        send_direct(0, 1, 0)

    def after_2():
        y_first(2)
        send_direct(0, 2, 1)
        send_relay(0, 1, 1)
        send_relay(0, 2, 0)

    def after_3():
        y_first(3)

    def after_4():
        send_far(1, 4)
        y_copy(0).wait_recv()
        send_far(2, 4)

    def after_5():
        send_direct(1, 5, 0)
        y_copy(1).wait_recv()
        send_direct(2, 5, 0)

    def after_6():
        send_direct(1, 6, 1)
        for half in (0, 1):
            yb_out[rows(x_span(0, half), B[0])] = total(0, 3, half).astype(BF16)
        yb_copy().start()

    betweens = [between_1, between_2, between_3]
    actions = [after_1, after_2, after_3, after_4, after_5, after_6]

    def dest(n):
        step = lax.rem(n, 4)
        dx = jnp.where(step == 0, 2, jnp.where(step == 1, 1, jnp.where(step == 2, 3, 0)))
        return lax.rem(yl + 1 + n // 4, 2) * 4 + lax.rem(x + dx, 4)

    def build(win, half, n):
        lag = pl.multiple_of(dest(n) * NS, NS)
        taps = TAPS[half]
        for b in range(NB):
            cols = slice(b * NS, (b + 1) * NS)
            for q in range(CG):
                wide = base[b * CG + q, :, pl.ds(lag, 512)].astype(BF16)
                scale = inv[b * CG + q, :, pl.ds(lag, NS)]
                for p in range(*PHASES[half]):
                    turned = pltpu.roll(wide, 512 - 4 * p, 1) if p else wide
                    turned = turned.astype(F32)
                    row = taps.index(p) * KR + q * 16
                    win[row : row + 16, cols] = (turned[:, :NS] * scale).astype(BF16)
                    if p + 32 in taps:
                        row = taps.index(p + 32) * KR + q * 16
                        win[row : row + 16, cols] = (
                            turned[:, 128 : 128 + NS] * scale).astype(BF16)

    build(win0, 0, 0)
    build(win1, 1, 0)
    part[0] = jnp.dot(lhs0[...], win0[...], preferred_element_type=F32)
    g_stage1(1)
    g_stage1(2)
    part[0] += jnp.dot(lhs1[...], win1[...], preferred_element_type=F32)
    after_0()
    g_finish(1)
    build(win0, 0, 1)

    def chunk(n, carry):
        build(win1, 1, n)
        part[n] = jnp.dot(lhs0[...], win0[...], preferred_element_type=F32)
        for m, action in enumerate(betweens):
            pl.when(n == m + 1)(action)
        build(win0, 0, jnp.minimum(n + 1, 7))
        part[n] += jnp.dot(lhs1[...], win1[...], preferred_element_type=F32)
        for m, action in enumerate(actions):
            pl.when(n == m + 1)(action)
        return carry

    lax.fori_loop(1, 8, chunk, 0)

    send_relay(1, 5, 1)
    send_relay(1, 6, 0)
    y_copy(2).wait_recv()
    send_direct(2, 6, 1)
    send_relay(2, 5, 1)
    send_relay(2, 6, 0)

    def finish(span, value):
        for b in range(NB):
            out_ref[b, rows(span)] = value[:, b * NS : (b + 1) * NS]

    y_copy(3).wait_recv()
    for half in (0, 1):
        finish(AH[half], total(2, 7, half))
    yb_copy().wait_recv()
    for half in (0, 1):
        span = x_span(1, half)
        finish(span, total(1, 7, half) + yb_in[rows(span, B[0])].astype(F32))

    for g in range(3):
        for m in range(15):
            g_copy(g, m).wait_send()
    for n in range(4):
        y_copy(n).wait_send()
    yb_copy().wait_send()
    for t in range(3):
        for kind in range(3):
            for half in (0, 1):
                x_copy(t, kind, half).wait_send()


def body(data, templates, counts, owners):
    vmem = pl.BlockSpec(memory_space=pltpu.VMEM)
    dma = pltpu.SemaphoreType.DMA
    traces = pl.pallas_call(
        kernel,
        out_shape=jax.ShapeDtypeStruct((NB, K, NS), F32),
        in_specs=[pl.BlockSpec(memory_space=pltpu.SMEM), vmem, pl.BlockSpec(memory_space=pl.ANY)],
        out_specs=vmem,
        scratch_shapes=[
            pltpu.VMEM((16, C, GROUPS[0]), BF16),
            pltpu.VMEM((16, C, GROUPS[1]), BF16),
            pltpu.VMEM((16, C, GROUPS[2]), BF16),
            pltpu.VMEM((2, W + 32, 128), F32),
            pltpu.VMEM((2, W * C + 8 * KR, 128), F32),
            pltpu.VMEM((K, KH[0]), BF16),
            pltpu.VMEM((K, KH[1]), BF16),
            pltpu.VMEM((NB * CG, 16, LB), F32),
            pltpu.VMEM((NB * CG, 16, LO), F32),
            pltpu.VMEM((512, NS), BF16),
            pltpu.VMEM((KH[0], NC), BF16),
            pltpu.VMEM((KH[1], NC), BF16),
            pltpu.VMEM((8, K, NC), F32),
            pltpu.VMEM((4, A[1], NC), BF16),
            pltpu.VMEM((4, A[1], NC), BF16),
            pltpu.VMEM((2, 3, K, NC), BF16),
            pltpu.VMEM((2, 3, K, NC), BF16),
            pltpu.VMEM((B[1] - B[0], NC), BF16),
            pltpu.VMEM((B[1] - B[0], NC), BF16),
            pltpu.VMEM((C + 1, W, K), BF16),
            dma(()),
            dma((3, 15)), dma((3, 15)), dma((5,)), dma((5,)), dma((18,)), dma((18,)),
        ],
        compiler_params=pltpu.CompilerParams(
            collective_id=0, has_side_effects=True, vmem_limit_bytes=60 << 20),
    )(owners, data[0], jnp.transpose(templates, (1, 2, 0)))
    live = jnp.arange(K, dtype=jnp.int32) < counts[0]
    return jnp.transpose(jnp.where(live[None, :, None], traces, 0.0), (1, 0, 2))


def solution(mesh):
    placed = (P("tmpl", "chan", None), P("tmpl", "chan", None), P("tmpl"), P())
    return jax.shard_map(
        body, mesh=mesh, in_specs=placed, out_specs=P("tmpl", None, "chan"), check_vma=False
    )
```

```python
import math

import jax
import jax.numpy as jnp
from jax import lax
from jax.experimental import pallas as pl
from jax.experimental.pallas import tpu as pltpu
from jax.sharding import PartitionSpec as P

W = 200
NB = 3
LO = 2048
C = 12
CG = C // 4
LB = 2304
K = 256
KR = 16 * CG
PHASES = ((0, 16), (16, 32))
TAPS = tuple(tuple(g for lo in (a, a + 32) for g in range(lo, lo + 16) if 4 * g < W) for a, _ in PHASES)
KH = tuple(len(taps) * KR for taps in TAPS)
NS = 256
NC = NB * NS
EPS = 1e-06
MESH = pl.DeviceIdType.MESH
GROUPS = (512, 1280, 1280)
MODES = ("chip", "chip", "tree")

A = (0, 112)
AH = ((0, 64), (64, 112))
B = (112, 256)
BH = ((192, 256), (112, 192))
F32 = jnp.float32
BF16 = jnp.bfloat16


def rows(span, base=0):
    return pl.ds(span[0] - base, span[1] - span[0])


def kernel(
    owners_ref, data_ref, tmpl_ref, out_ref,
    arch0, arch1, arch2, normed, columns, lhs0, lhs1, base, inv, band, win0, win1, part,
    y_out, y_in, xo, xi, yb_out, yb_in, held, held_sem,
    g_send, g_recv, y_send, y_recv, x_send, x_recv,
):
    tm = lax.axis_index("tmpl")
    ch = lax.axis_index("chan")
    z, yh, core = tm // 4, lax.rem(tm // 2, 2), lax.rem(tm, 2)
    yl, x = ch // 4, lax.rem(ch, 4)
    e = 1 - 2 * core

    def block(dz, dyh):
        return lax.rem(z + 4 + dz * e, 4) * 4 + lax.rem(yh + dyh, 2) * 2 + core

    def holder(dz, dyh, dcore):
        near = lax.rem(z + dz, 4) * 4 + lax.rem(yh + dyh, 2) * 2 + lax.rem(core + dcore, 2)
        return {"tmpl": near, "chan": ch}

    def chan_at(dyl, dx):
        return lax.rem(yl + dyl, 2) * 4 + lax.rem(x + dx, 4)

    ahead = {"tmpl": block(1, 0), "chan": ch}
    behind = {"tmpl": block(-1, 0), "chan": ch}
    across = {"tmpl": block(0, 1), "chan": ch}
    mate = holder(0, 0, 1)
    x_dev = {-1: {"tmpl": tm, "chan": chan_at(0, 3)}, 1: {"tmpl": tm, "chan": chan_at(0, 1)}}
    y_dev = {"tmpl": tm, "chan": chan_at(1, 0)}

    fetch = pltpu.make_async_copy(tmpl_ref, held.at[pl.ds(0, C)], held_sem)
    fetch.start()
    barrier = pltpu.get_barrier_semaphore()
    chips = [(dz, dyh) for dyh in range(2) for dz in (2, 1, 3, 0) if dz or dyh]
    others = [holder(dz, dyh, dcore) for dcore in range(2) for dz, dyh in chips] + [mate]
    peers = others[:7] + [mate, y_dev, x_dev[-1], x_dev[1]]
    for peer in peers:
        pl.semaphore_signal(barrier, inc=1, device_id=peer, device_id_type=MESH)
    pl.semaphore_wait(barrier, len(peers))

    def remote(src, dst, send, recv, device):
        return pltpu.make_async_remote_copy(
            src, dst, send, recv, device_id=device, device_id_type=MESH)

    archs = (arch0, arch1, arch2)
    first = (1 - yl) * 4 + lax.rem(x + 2, 4)
    starts = [
        pl.multiple_of(first * NS, NS),
        pl.multiple_of((1 - yl) * 1024, 1024),
        pl.multiple_of(yl * 1024, 1024),
    ]
    tree_targets = (ahead, behind, across, ahead, ahead, behind, ahead, mate) + (mate,) * 7
    carried = (None, None, None, (-1, 0), (0, 1), (0, 1), (-1, 1), None)
    carried += ((-1, 0), (1, 0), (0, 1), (-2, 0), (-1, 1), (1, 1), (-2, 1))

    def g_copy(g, m):
        mode = MODES[g]
        source = None
        if mode == "all":
            target = others[m]
        elif mode == "chip":
            target = others[m] if m < 7 else mate
            if m > 7:
                dz, dyh = chips[m - 8]
                source = holder((4 - dz) % 4, dyh, 0)["tmpl"]
        else:
            target = tree_targets[m]
            if carried[m] is not None:
                source = block(*carried[m])
        if source is None:
            src = data_ref.at[:, pl.ds(starts[g], GROUPS[g])]
            dst = archs[g].at[tm]
        else:
            src = dst = archs[g].at[source]
        return remote(src, dst, g_send.at[g, m], g_recv.at[g, m], target)

    def g_start(g):
        first = {"all": range(15), "chip": range(8), "tree": (2, 0, 1, 7)}[MODES[g]]
        for m in first:
            g_copy(g, m).start()
        archs[g][tm] = data_ref[:, pl.ds(starts[g], GROUPS[g])]

    def g_pass(g, m, on):
        g_copy(g, m).wait_recv()
        for k in on:
            g_copy(g, k).start()

    def g_stage1(g):
        if MODES[g] == "tree":
            g_pass(g, 0, (3, 8))
            g_pass(g, 1, (9,))
            g_pass(g, 2, (4, 5, 10))
        if MODES[g] == "chip":
            for m in (6, 1, 2, 0, 4, 5, 3):
                g_pass(g, m, (8 + m,))

    def g_stage2(g):
        if MODES[g] == "tree":
            g_pass(g, 3, (11,))
            g_pass(g, 4, (6, 12))
            g_pass(g, 5, (13,))

    def g_stage3(g):
        if MODES[g] == "tree":
            g_pass(g, 6, (14,))

    def g_finish(g):
        for m in range(0 if MODES[g] == "all" else 7, 15):
            g_copy(g, m).wait_recv()
        width = GROUPS[g]
        for b in range(NB):
            seg = archs[g][owners_ref[b]].astype(F32)
            seg = jnp.concatenate([seg, jnp.zeros((4, width), F32)], axis=0)
            small = seg * (1.0 / 256)
            power = jnp.minimum(small * small, 2.0**120)
            high = power.astype(BF16)
            low = (power - high.astype(F32)).astype(BF16)
            squares = jnp.concatenate([high, low], axis=0)
            for n in range(width // NS - 1):
                energy = jnp.dot(squares[:, n * NS : n * NS + 512], band[...],
                                 preferred_element_type=F32)
                mean = (energy[:16] + energy[16:]) * (65536.0 / W)
                scale = 1.0 / (jnp.sqrt(mean + EPS) * math.sqrt(W))
                for q in range(CG):
                    for s in range(4):
                        inv[b * CG + q, 4 * s : 4 * s + 4, pl.ds(starts[g] + n * NS, NS)] = (
                            scale[4 * q : 4 * q + 4])
            seg = seg.astype(BF16)
            for s in range(4):
                turned = pltpu.roll(seg, width - s, 1) if s else seg
                turned = turned.astype(F32)
                for q in range(CG):
                    base[b * CG + q, 4 * s : 4 * s + 4, pl.ds(starts[g], width)] = (
                        turned[4 * q : 4 * q + 4])

    g_start(0)
    g_start(2)
    g_start(1)

    sample = lax.broadcasted_iota(jnp.int32, (512, NS), 0)
    lag_of = lax.broadcasted_iota(jnp.int32, (512, NS), 1)
    inside = jnp.logical_and(sample >= lag_of, sample < lag_of + W)
    band[...] = jnp.where(inside, 1.0, 0.0).astype(BF16)

    fetch.wait()
    for c in range(C):
        values = held[c].astype(F32)
        power = jnp.sum(values * values, axis=0, keepdims=True) * (1.0 / W)
        scaled = values * (1.0 / (jnp.sqrt(power + EPS) * math.sqrt(W)))
        for j in range(2):
            normed[j, :W] = scaled[:, j * 128 : j * 128 + 128]
            for s in range(4):
                row = c // 4 * 16 + 4 * s + c % 4
                columns[j, pl.ds(row, W // 4, stride=KR), :] = (
                    normed[j, pl.ds(s, W // 4, stride=4), :])
    for lhs, (lo, hi) in ((lhs0, PHASES[0]), (lhs1, PHASES[1])):
        tail = min(hi + 32, W // 4)
        for j in range(2):
            band_rows = slice(j * 128, j * 128 + 128)
            cut = (hi - lo) * KR
            lhs[band_rows, :cut] = columns[j, lo * KR : hi * KR, :].T.astype(BF16)
            lhs[band_rows, cut:] = columns[j, (lo + 32) * KR : tail * KR, :].T.astype(BF16)

    g_stage1(0)
    g_stage2(0)
    g_stage3(0)
    g_finish(0)

    def y_copy(n):
        return remote(y_out.at[n], y_in.at[n], y_send.at[n], y_recv.at[n], y_dev)

    def yb_copy():
        return remote(yb_out, yb_in, y_send.at[4], y_recv.at[4], y_dev)

    def x_span(t, half):
        return AH[half] if t == 2 else BH[half]

    def x_slot(t):
        return t % 2

    def x_copy(t, kind, half):
        span = rows(x_span(t, half))
        direction = -1 if half == 0 else 1
        if kind == 2:
            direction = -direction
        n = (t * 3 + kind) * 2 + half
        return remote(
            xo.at[x_slot(t), kind, span], xi.at[x_slot(t), kind, span],
            x_send.at[n], x_recv.at[n], x_dev[direction])

    def x_put(t, kind, half, value):
        xo[x_slot(t), kind, rows(x_span(t, half))] = value.astype(BF16)
        x_copy(t, kind, half).start()

    def x_got(t, kind, half):
        x_copy(t, kind, half).wait_recv()
        return xi[x_slot(t), kind, rows(x_span(t, half))].astype(F32)

    def own(n, span):
        return part[n, rows(span)]

    def local(t, n, half):
        span = x_span(t, half)
        if t == 2:
            return own(n, span) + y_in[n - 4, rows(span)].astype(F32)
        return own(n, span)

    def send_far(t, n):
        for half in (0, 1):
            x_put(t, 0, half, local(t, n, half))

    def send_direct(t, n, half):
        x_put(t, 2, half, local(t, n, half))

    def send_relay(t, n, half):
        x_put(t, 1, half, local(t, n, half) + x_got(t, 0, half))

    def total(t, n, half):
        return local(t, n, half) + x_got(t, 1, half) + x_got(t, 2, half)

    def y_first(n):
        y_out[n] = own(n, A).astype(BF16)
        y_copy(n).start()

    def between_1():
        g_stage2(2)

    def between_2():
        g_stage3(2)

    def between_3():
        g_finish(2)

    def after_0():
        y_first(0)
        send_far(0, 0)

    def after_1():
        y_first(1)
        send_direct(0, 1, 0)

    def after_2():
        y_first(2)
        send_direct(0, 2, 1)
        send_relay(0, 1, 1)
        send_relay(0, 2, 0)

    def after_3():
        y_first(3)

    def after_4():
        send_far(1, 4)
        y_copy(0).wait_recv()
        send_far(2, 4)

    def after_5():
        send_direct(1, 5, 0)
        y_copy(1).wait_recv()
        send_direct(2, 5, 0)

    def after_6():
        send_direct(1, 6, 1)
        for half in (0, 1):
            yb_out[rows(x_span(0, half), B[0])] = total(0, 3, half).astype(BF16)
        yb_copy().start()

    betweens = [between_1, between_2, between_3]
    actions = [after_1, after_2, after_3, after_4, after_5, after_6]

    def dest(n):
        step = lax.rem(n, 4)
        dx = jnp.where(step == 0, 2, jnp.where(step == 1, 1, jnp.where(step == 2, 3, 0)))
        return lax.rem(yl + 1 + n // 4, 2) * 4 + lax.rem(x + dx, 4)

    def build(win, half, n):
        lag = pl.multiple_of(dest(n) * NS, NS)
        taps = TAPS[half]
        for b in range(NB):
            cols = slice(b * NS, (b + 1) * NS)
            for q in range(CG):
                wide = base[b * CG + q, :, pl.ds(lag, 512)].astype(BF16)
                scale = inv[b * CG + q, :, pl.ds(lag, NS)]
                for p in range(*PHASES[half]):
                    turned = pltpu.roll(wide, 512 - 4 * p, 1) if p else wide
                    turned = turned.astype(F32)
                    row = taps.index(p) * KR + q * 16
                    win[row : row + 16, cols] = (turned[:, :NS] * scale).astype(BF16)
                    if p + 32 in taps:
                        row = taps.index(p + 32) * KR + q * 16
                        win[row : row + 16, cols] = (
                            turned[:, 128 : 128 + NS] * scale).astype(BF16)

    build(win0, 0, 0)
    build(win1, 1, 0)
    part[0] = jnp.dot(lhs0[...], win0[...], preferred_element_type=F32)
    g_stage1(1)
    g_stage1(2)
    part[0] += jnp.dot(lhs1[...], win1[...], preferred_element_type=F32)
    after_0()
    g_finish(1)
    build(win0, 0, 1)

    def chunk(n, carry):
        build(win1, 1, n)
        part[n] = jnp.dot(lhs0[...], win0[...], preferred_element_type=F32)
        for m, action in enumerate(betweens):
            pl.when(n == m + 1)(action)
        build(win0, 0, jnp.minimum(n + 1, 7))
        part[n] += jnp.dot(lhs1[...], win1[...], preferred_element_type=F32)
        for m, action in enumerate(actions):
            pl.when(n == m + 1)(action)
        return carry

    lax.fori_loop(1, 8, chunk, 0)

    send_relay(1, 5, 1)
    send_relay(1, 6, 0)
    y_copy(2).wait_recv()
    send_direct(2, 6, 1)
    send_relay(2, 5, 1)
    send_relay(2, 6, 0)

    def finish(span, value):
        for b in range(NB):
            out_ref[b, rows(span)] = value[:, b * NS : (b + 1) * NS]

    yb_copy().wait_recv()
    for half in (0, 1):
        span = x_span(1, half)
        finish(span, total(1, 7, half) + yb_in[rows(span, B[0])].astype(F32))
    y_copy(3).wait_recv()
    for half in (0, 1):
        finish(AH[half], total(2, 7, half))

    for g in range(3):
        for m in range(15):
            g_copy(g, m).wait_send()
    for n in range(4):
        y_copy(n).wait_send()
    yb_copy().wait_send()
    for t in range(3):
        for kind in range(3):
            for half in (0, 1):
                x_copy(t, kind, half).wait_send()


def body(data, templates, counts, owners):
    vmem = pl.BlockSpec(memory_space=pltpu.VMEM)
    dma = pltpu.SemaphoreType.DMA
    traces = pl.pallas_call(
        kernel,
        out_shape=jax.ShapeDtypeStruct((NB, K, NS), F32),
        in_specs=[pl.BlockSpec(memory_space=pltpu.SMEM), vmem, pl.BlockSpec(memory_space=pl.ANY)],
        out_specs=vmem,
        scratch_shapes=[
            pltpu.VMEM((16, C, GROUPS[0]), BF16),
            pltpu.VMEM((16, C, GROUPS[1]), BF16),
            pltpu.VMEM((16, C, GROUPS[2]), BF16),
            pltpu.VMEM((2, W + 32, 128), F32),
            pltpu.VMEM((2, W * C + 8 * KR, 128), F32),
            pltpu.VMEM((K, KH[0]), BF16),
            pltpu.VMEM((K, KH[1]), BF16),
            pltpu.VMEM((NB * CG, 16, LB), F32),
            pltpu.VMEM((NB * CG, 16, LO), F32),
            pltpu.VMEM((512, NS), BF16),
            pltpu.VMEM((KH[0], NC), BF16),
            pltpu.VMEM((KH[1], NC), BF16),
            pltpu.VMEM((8, K, NC), F32),
            pltpu.VMEM((4, A[1], NC), BF16),
            pltpu.VMEM((4, A[1], NC), BF16),
            pltpu.VMEM((2, 3, K, NC), BF16),
            pltpu.VMEM((2, 3, K, NC), BF16),
            pltpu.VMEM((B[1] - B[0], NC), BF16),
            pltpu.VMEM((B[1] - B[0], NC), BF16),
            pltpu.VMEM((C + 1, W, K), BF16),
            dma(()),
            dma((3, 15)), dma((3, 15)), dma((5,)), dma((5,)), dma((18,)), dma((18,)),
        ],
        compiler_params=pltpu.CompilerParams(
            collective_id=0, has_side_effects=True, vmem_limit_bytes=60 << 20),
    )(owners, data[0], jnp.transpose(templates, (1, 2, 0)))
    live = jnp.arange(K, dtype=jnp.int32) < counts[0]
    return jnp.transpose(jnp.where(live[None, :, None], traces, 0.0), (1, 0, 2))


def solution(mesh):
    placed = (P("tmpl", "chan", None), P("tmpl", "chan", None), P("tmpl"), P())
    return jax.shard_map(
        body, mesh=mesh, in_specs=placed, out_specs=P("tmpl", None, "chan"), check_vma=False
    )
```
